128 devices in a mesh: arc: 16 (over x, z), vec: 8 (over y, core).
Axes of the slice: x: 4, y: 4, z: 4, core: 2. Of those that a mesh axis runs over, the one named last changes fastest.
Arguments:
- right_side: float32 [640, 128, 128], P(('arc', 'vec')), may hold values from -6 to 6
- prior_diag: float32 [640, 128], P(('arc', 'vec')), may hold values from 0.5 to 4
- inv_factor: bfloat16 [2048, 256, 256], P(('arc', 'vec'))
- coupling_panel: bfloat16 [2048, 256, 1024], P(('arc', 'vec')), may hold values from -0.09375 to 0.09375
- coupling_owner: int32 [2048, 8], replicated, may hold values from 0 to 127, all different within a row; in each aligned block of 16 rows (0 to 15, 16 to 31, ...) at most 2 rows name the same one
- coupling_block: int32 [2048, 8], replicated, may hold values from 0 to 4
Outputs:
- solution_field: float32 [640, 128, 128], P(('arc', 'vec'))
- residual: float32 [640, 128, 128], P(('arc', 'vec'))
The draws below stay inside these ranges and needn't reach their ends.
Inputs may be any that keep to these rules, and one draw needn't show every extreme that they name: `coupling_owner`: the 8 holders named for one arc are different. Among the 16 arcs of one device (aligned blocks of rows) no holder is named more than 2 times; some holder is named exactly 2 times.
All inputs are finite; a program needn't handle non-finite values.
Results may differ from the reference program's by a relative error of at most 0.006.
The reference program's roundings to bfloat16 on the way count: a program that leaves them out, or rounds other values in their place, can miss the bound.
Values may be sent and summed in bfloat16 or wider, within the bound.
A program may use at most 128 MiB of HBM per device.

```python
import math
import jax
import jax.numpy as jnp
import numpy as np
from jax import lax

BR = 128
GBLK = 640
AP = 256
RHS = 128
K = 8
ITERS = 2
ARC_DEV = 16
ARCS = 2048
BLK_DEV = 5
CAP = 2
DEVICES = 128


def draw_inv_factor(key, part):
    key_diag, key_below = jax.random.split(key)
    diagonal_part = jax.random.uniform(key_diag, (ARCS, AP), jnp.float32, 0.7, 1.3)
    below_part = jax.random.normal(key_below, (ARCS, AP, AP), jnp.float32) * (0.5 / math.sqrt(AP))
    strict_lower = jnp.tril(jnp.ones((AP, AP), jnp.float32), -1)
    identity = jnp.eye(AP, dtype=jnp.float32)
    full_factor = below_part * strict_lower[None] + diagonal_part[:, :, None] * identity[None]
    return full_factor.astype(jnp.bfloat16)


def place_ends(array, stream_key, low, largest):
    longest = array.shape.index(max(array.shape))
    spots = []
    for shift in (0, 1):
        where = [jax.random.randint(jax.random.fold_in(stream_key, axis), (), 0, length) for axis, length in enumerate(array.shape)]
        where[longest] = (where[longest] + shift) % array.shape[longest]
        spots.append(tuple(where))
    return array.at[spots[0]].set(low).at[spots[1]].set(largest)


def block_scale(rng, dims, cuts, least, top_value):
    level = 1.0
    for dim, parts in cuts:
        draws = jax.random.uniform(jax.random.fold_in(jax.random.fold_in(rng, 6), dim), (parts,), jnp.float32, least / len(cuts), top_value / len(cuts))
        level = level * jnp.repeat(jnp.exp(draws), dims[dim] // parts).reshape((-1,) + (1,) * (len(dims) - 1 - dim))
    return level


def routed_block(rng, own, number, rows, count, top, reach, skew):
    ranking = jax.random.permutation(rng, count)
    heavy_load, usual = shares(count, rows * top, reach, skew, True), shares(count, rows * top, reach, skew, False)
    places = jnp.arange(count)

    def named(lengths, turn):
        used = int((lengths > 0).sum())
        fixed = max(1, used // 4)
        passed = fixed + (places - fixed + turn * (used - fixed)) % max(1, count - fixed)
        return jnp.zeros((count,), jnp.int32).at[ranking[jnp.where(places < fixed, places, passed)]].set(jnp.asarray(lengths, jnp.int32))

    lengths = jnp.where(number % 4 == 0, named(heavy_load, number // 4), named(usual, number - number // 4 - 1))
    mixed = jax.random.permutation(jax.random.fold_in(own, 3), count)
    giver, taker = mixed[0:count // 2 * 2:2], mixed[1:count // 2 * 2:2]
    slack = jnp.minimum(lengths[giver] - 1, reach - lengths[taker]) // 2
    slack = jnp.where((giver == ranking[0]) | (taker == ranking[0]) | (lengths[taker] == 0), 0, jnp.maximum(slack, 0))
    passed = jax.random.randint(jax.random.fold_in(own, 4), (count // 2,), 0, 1 << 20) % (slack + 1)
    lengths = lengths.at[giver].add(-passed).at[taker].add(passed)
    labels = jnp.searchsorted(jnp.cumsum(lengths), jnp.arange(rows * top), side="right").astype(jnp.int32)
    listing = labels.reshape(top, rows).T
    listing = listing[jax.random.permutation(jax.random.fold_in(own, 1), rows)]
    turn = jax.random.randint(jax.random.fold_in(own, 2), (rows, 1), 0, top)
    return jnp.take_along_axis(listing, (jnp.arange(top)[None, :] + turn) % top, axis=1)


def shares(amount, total, reach, skew, full):
    weights = [(1 << 20) // math.isqrt(grade ** skew) + 1 for grade in range(1, amount + 1)]
    largest = reach if full else min(reach, max(-(-total // amount), total * weights[0] // sum(weights)))
    least = 1 if total - largest >= amount - 1 else 0
    holding, surplus = [largest] + [least] * (amount - 1), total - largest - least * (amount - 1)
    while surplus > 0:
        candidates = [i for i in range(1, amount) if holding[i] < largest] or [i for i in range(1, amount) if holding[i] < reach]
        whole, left = sum([weights[i] for i in candidates]), surplus
        for i in candidates:
            extra = min(reach - holding[i], max(1, left * weights[i] // whole), surplus)
            holding[i] = holding[i] + extra
            surplus = surplus - extra
    return np.array(holding)


def bell_draw(key, shape, width, reach, cuts=(), kind=jnp.bfloat16):
    level = block_scale(key, shape, cuts, -0.22, 0.18) if cuts else 1.0
    array = jax.random.normal(key, shape, jnp.float32) * width * level
    return jnp.minimum(jnp.maximum(array, -reach), reach).astype(kind)


def setup_inputs(seed: int = 0) -> dict:
    seeds = jax.random.split(jax.random.key(seed), 7)
    right_side = bell_draw(seeds[0], (GBLK, BR, RHS), 1.0, 6.0, ((0, 128),), jnp.float32)
    prior_diag = jnp.clip(jnp.exp(math.log(4.0) - 2.0794415 * jax.random.uniform(seeds[1], (GBLK, BR), jnp.float32) ** block_scale(seeds[1], (GBLK, BR), ((0, 128),), -0.2, 0.2)), 0.5, 4.0)
    inv_factor = draw_inv_factor(jax.random.fold_in(seeds[6], 71), 0)
    coupling_panel = bell_draw(seeds[3], (ARCS, AP, K * BR), (K * BR * 4) ** -0.5, 0.09375, ((0, 128),))
    coupling_owner_keys = jax.random.split(jax.random.fold_in(seeds[4], 1), ARCS // ARC_DEV)
    coupling_owner_turns = jax.random.permutation(jax.random.fold_in(seeds[4], 3), ARCS // ARC_DEV)
    coupling_owner = jax.vmap(lambda own, number: routed_block(jax.random.fold_in(seeds[4], 2), own, number, ARC_DEV, DEVICES, K, CAP, 2))(coupling_owner_keys, coupling_owner_turns).reshape((ARCS, K))
    coupling_block = place_ends(jax.random.randint(seeds[5], (ARCS, K), 0, BLK_DEV), jax.random.fold_in(seeds[5], 1), 0, BLK_DEV - 1).astype(jnp.int32)
    return {"right_side": right_side, "prior_diag": prior_diag, "inv_factor": inv_factor, "coupling_panel": coupling_panel, "coupling_owner": coupling_owner, "coupling_block": coupling_block}


def round_bf16(values):
    return lax.optimization_barrier(values.astype(jnp.bfloat16)).astype(jnp.float32)

def inner_gram(left, right):
    return jnp.einsum('grc,grd->cd', left, right, precision=lax.Precision.HIGHEST)

def combine_cols(field, weights):
    return jnp.einsum('grc,cd->grd', field, weights, precision=lax.Precision.HIGHEST)

def apply_schur(field, prior_diag, inv_factor, coupling_panel, global_index):
    rounded = round_bf16(field)
    factor_groups = inv_factor.reshape(DEVICES, ARC_DEV, AP, AP)
    panel_groups = coupling_panel.reshape(DEVICES, ARC_DEV, AP, K * BR)
    index_groups = global_index.reshape(DEVICES, ARC_DEV * K)

    def arc_group(summed, group_data):
        factor_part, panel_part, group_index = group_data
        factor_f32 = factor_part.astype(jnp.float32)
        panel_f32 = panel_part.astype(jnp.float32)
        fetched = rounded[group_index].reshape(ARC_DEV, K * BR, RHS)
        coupled = round_bf16(jnp.einsum('apk,akc->apc', panel_f32, fetched, precision=lax.Precision.HIGHEST))
        whitened = round_bf16(jnp.einsum('apq,aqc->apc', factor_f32, coupled, precision=lax.Precision.HIGHEST))
        smoothed = round_bf16(jnp.einsum('aqp,aqc->apc', factor_f32, whitened, precision=lax.Precision.HIGHEST))
        projected = round_bf16(jnp.einsum('apk,apc->akc', panel_f32, smoothed, precision=lax.Precision.HIGHEST))
        summed = summed.at[group_index].add(projected.reshape(ARC_DEV * K, BR, RHS))
        return (summed, None)
    start = jnp.zeros((GBLK, BR, RHS), jnp.float32)
    summed, _ = lax.scan(arc_group, start, (factor_groups, panel_groups, index_groups))
    return prior_diag[:, :, None] * field + summed

def reference(right_side, prior_diag, inv_factor, coupling_panel, coupling_owner, coupling_block):
    global_index = (coupling_owner * BLK_DEV + coupling_block).astype(jnp.int32)
    solution_field = jnp.zeros_like(right_side)
    residual = right_side
    direction = right_side
    res_gram = inner_gram(residual, residual)
    for sweep_index in range(ITERS):
        image_vec = apply_schur(direction, prior_diag, inv_factor, coupling_panel, global_index)
        curv_gram = inner_gram(direction, image_vec)
        factor_low = jnp.linalg.cholesky(curv_gram)
        step_mat = jax.scipy.linalg.cho_solve((factor_low, True), res_gram)
        solution_field = solution_field + combine_cols(direction, step_mat)
        residual = residual - combine_cols(image_vec, step_mat)
        if sweep_index + 1 < ITERS:
            new_gram = inner_gram(residual, residual)
            beta_mat = jax.scipy.linalg.cho_solve((jnp.linalg.cholesky(res_gram), True), new_gram)
            direction = residual + combine_cols(direction, beta_mat)
            res_gram = new_gram
    return (solution_field, residual)
```

```python
import functools
import jax
import jax.numpy as jnp
from jax import lax
from jax.experimental import pallas as pl
from jax.experimental.pallas import tpu as pltpu
from jax.sharding import PartitionSpec as P
MESH = pl.DeviceIdType.MESH
DIMS = ((0, 1, 2), (1, 2, 0), (2, 0, 1))
CUT = ((0, 112, 208), (208, 320, 432), (432, 528, 640))
OFFS = (0, 3, 1, 2)

def coords():
    arc, vec = lax.axis_index("arc"), lax.axis_index("vec")
    return (arc // 4, arc % 4, vec // 2), vec % 2

def dev(pos, core):
    return (pos[0] * 4 + pos[1], pos[2] * 2 + core)

def moved(pos, dim, off):
    return tuple((p + off) % 4 if d == dim else p for d, p in enumerate(pos))

def entry_barrier(pos, core):
    barrier = pltpu.get_barrier_semaphore()
    for dim in range(3):
        for off in (1, 3):
            pl.semaphore_signal(barrier, inc=1, device_id=dev(moved(pos, dim, off), core), device_id_type=MESH)
    pl.semaphore_signal(barrier, inc=1, device_id=dev(pos, 1 - core), device_id_type=MESH)
    pl.semaphore_wait(barrier, 7)

def gather_all(G, send, recv, csend, crecv, pos, core):
    pend = []
    cpend = []
    nsem = [0]
    ncs = [0]
    def at(sel, cc, rows):
        return G.at[sel[0], sel[1], sel[2], cc, pl.ds(rows[0], rows[1] - rows[0])]
    def make(sel_src, dim, off, rows):
        i = nsem[0]; nsem[0] += 1
        ref = at(sel_src, core, rows)
        return pltpu.make_async_remote_copy(ref, ref, send.at[i], recv.at[i],
            device_id=dev(moved(pos, dim, off), core), device_id_type=MESH)
    def start(sel, dim, off, rows):
        c = make(sel, dim, off, rows); c.start(); pend.append(c); return c
    def cross(sel, rows):
        i = ncs[0]; ncs[0] += 1
        ref = at(sel, core, rows)
        c = pltpu.make_async_remote_copy(ref, ref, csend.at[i], crecv.at[i],
            device_id=dev(pos, 1 - core), device_id_type=MESH)
        c.start(); cpend.append(c)
    def rel(dim, off):
        return moved(pos, dim, off)
    def allof(sel, *dims):
        return tuple(slice(None) if d in dims else s for d, s in enumerate(sel))
    A = [(c[0], c[1]) for c in CUT]; B = [(c[1], c[2]) for c in CUT]; F = [(c[0], c[2]) for c in CUT]
    s1 = {}; f1 = {}; s2 = {}; f2 = {}; s3 = {}; f3 = {}
    def S2(p, o1):
        d1, d2, d3 = DIMS[p]
        for off in (1, 3):
            s2[p, o1, off] = start(moved(pos, d1, o1), d2, off, F[p])
    def S3(p, o2):
        d1, d2, d3 = DIMS[p]
        for off in (1, 3):
            s3[p, o2, off] = start(allof(moved(pos, d2, o2), d1), d3, off, F[p])
    for p in range(3):
        d1 = DIMS[p][0]
        for off in (1, 3):
            s1[p, off] = start(pos, d1, off, F[p])
    for p in range(3):
        S2(p, 0)
    cross(pos, (0, 640))
    for p in range(3):
        d1 = DIMS[p][0]
        s1[p, 1].wait_recv()
        f1[p, 1] = start(rel(d1, 3), d1, 1, A[p])
        s1[p, 3].wait_recv()
        f1[p, 3] = start(rel(d1, 1), d1, 3, B[p])
    for p in range(3):
        S2(p, 3); S2(p, 1)
        d1 = DIMS[p][0]
        cross(rel(d1, 3), F[p]); cross(rel(d1, 1), F[p])
    for p in range(3):
        f1[p, 1].wait_recv(); f1[p, 3].wait_recv()
        S2(p, 2)
        S3(p, 0)
        cross(rel(DIMS[p][0], 2), F[p])
    for o1 in OFFS:
        for p in range(3):
            d1, d2, d3 = DIMS[p]
            s2[p, o1, 1].wait_recv()
            f2[p, o1, 1] = start(moved(rel(d1, o1), d2, 3), d2, 1, A[p])
            s2[p, o1, 3].wait_recv()
            f2[p, o1, 3] = start(moved(rel(d1, o1), d2, 1), d2, 3, B[p])
    for p in range(3):
        d1, d2, d3 = DIMS[p]
        S3(p, 3); S3(p, 1)
        cross(allof(rel(d2, 3), d1), F[p]); cross(allof(rel(d2, 1), d1), F[p])
    for p in range(3):
        d1, d2, d3 = DIMS[p]
        for o1 in OFFS:
            f2[p, o1, 1].wait_recv(); f2[p, o1, 3].wait_recv()
        S3(p, 2)
        cross(allof(rel(d2, 2), d1), F[p])
    for o2 in OFFS:
        for p in range(3):
            d1, d2, d3 = DIMS[p]
            s3[p, o2, 1].wait_recv()
            sel = allof(moved(rel(d2, o2), d3, 3), d1)
            f3[p, o2, 1] = start(sel, d3, 1, A[p])
            cross(sel, F[p])
            s3[p, o2, 3].wait_recv()
            sel = allof(moved(rel(d2, o2), d3, 1), d1)
            f3[p, o2, 3] = start(sel, d3, 3, B[p])
            cross(sel, F[p])
    for o2 in OFFS:
        for p in range(3):
            d1, d2, d3 = DIMS[p]
            f3[p, o2, 1].wait_recv(); f3[p, o2, 3].wait_recv()
            cross(allof(moved(rel(d2, o2), d3, 2), d1), F[p])
    for c in cpend:
        c.wait_recv()
    for c in pend + cpend:
        c.wait_send()
    return nsem[0], ncs[0]

NS, NC = 108, 55


ORDER = (2, 1, 3, 0)
F32, BF16 = jnp.float32, jnp.bfloat16
FULL = [(c[0], c[2]) for c in CUT]; HA = [(c[0], c[1]) for c in CUT]; HB = [(c[1], c[2]) for c in CUT]

def barrier_all(pos, core, far):
    barrier = pltpu.get_barrier_semaphore()
    offs = (1, 2, 3) if far else (1, 3)
    for dim in range(3):
        for off in offs:
            pl.semaphore_signal(barrier, inc=1, device_id=dev(moved(pos, dim, off), core), device_id_type=MESH)
    pl.semaphore_signal(barrier, inc=1, device_id=dev(pos, 1 - core), device_id_type=MESH)
    pl.semaphore_wait(barrier, 3 * len(offs) + 1)

def pieces(p):
    lo, hi = FULL[p]
    out = []
    for b in range(5):
        r0, r1 = max(lo, b * 128), min(hi, b * 128 + 128)
        if r0 < r1:
            out.append((b, r0 - b * 128, r1 - b * 128))
    return out

def rows(r):
    return pl.ds(r[0], r[1] - r[0])

def reduce_scatter(proj, tab, H, W, FR, SR, send, recv, pos, core):
    count = [0]
    pend = []
    tags = {}
    def ring_dim(p, lvl):
        return DIMS[p][2 - lvl]
    def hsel(p, lvl, grp, off):
        d1, d2, d3 = DIMS[p]
        sel = list(pos)
        if lvl == 0:
            sel[d1] = slice(None); sel[d2] = (pos[d2] + grp) % 4; sel[d3] = (pos[d3] + off) % 4
        elif lvl == 1:
            sel[d1] = (pos[d1] + grp) % 4; sel[d2] = (pos[d2] + off) % 4
        else:
            sel[d1] = (pos[d1] + off) % 4
        return tuple(sel)
    def rsel(p, lvl, grp):
        d1, d2, d3 = DIMS[p]
        if lvl == 0:
            return tuple(slice(None) if d == d1 else (pos[d2] + grp) % 4 for d in sorted((d1, d2)))
        if lvl == 1:
            return ((pos[d1] + grp) % 4,)
        return ()
    def wsel(p, lvl, grp, off):
        h = hsel(p, lvl, grp, off)
        return tuple(h[d] for d in sorted(DIMS[p][:2]))
    def source(p, lvl, grp, off, rr):
        if lvl == 0:
            return H.at[(*hsel(p, lvl, grp, off), rows(rr))]
        return W.at[(*wsel(p, lvl, grp, off), rows(rr))]
    def start(src, dst, p, lvl, off, tag):
        i = count[0]; count[0] += 1
        c = pltpu.make_async_remote_copy(src, dst, send.at[i], recv.at[i],
            device_id=dev(moved(pos, ring_dim(p, lvl), off), core), device_id_type=MESH)
        c.start(); pend.append(c); tags[tag] = c
    def send_f(p, lvl, grp):
        r = rsel(p, lvl, grp)
        start(source(p, lvl, grp, 2, HA[p]), FR[lvl].at[(*r, rows(HA[p]))], p, lvl, 1, ("f", p, lvl, grp, 1))
        start(source(p, lvl, grp, 2, HB[p]), FR[lvl].at[(*r, rows(HB[p]))], p, lvl, 3, ("f", p, lvl, grp, 3))
    def send_s(p, lvl, grp, off, half):
        r = rsel(p, lvl, grp)
        rr = (HA if half == 0 else HB)[p]
        start(source(p, lvl, grp, off, rr), SR[lvl].at[(0 if off == 1 else 1, *r, rows(rr))], p, lvl, off, ("s", p, lvl, grp, off, half))
    def chunks(h, r, body):
        if any(isinstance(s, slice) for s in h):
            def step(i, _):
                body(tuple(i if isinstance(s, slice) else s for s in h), tuple(i if isinstance(s, slice) else s for s in r))
                return 0
            lax.fori_loop(0, 4, step, 0)
        else:
            body(h, r)
    def fill(p, grp, off):
        def body(h, r):
            g0 = ((h[0] * 4 + h[1]) * 8 + h[2] * 2 + core) * 5
            for b, r0, r1 in pieces(p):
                rr = pl.ds(r0, r1 - r0)
                e = [tab[(g0 + b) * 4 + k] for k in range(4)]
                v = (proj[e[0], rr] + proj[e[1], rr]) + (proj[e[2], rr] + proj[e[3], rr])
                H[(*h, pl.ds(b * 128 + r0, r1 - r0))] = v
        h = hsel(p, 0, grp, off)
        chunks(h, h, body)
    def add_f(p, lvl, grp, off):
        rr = rows((HA if off == 1 else HB)[p])
        def body(h, r):
            if lvl == 0:
                H[(*h, rr)] = (H[(*h, rr)].astype(F32) + FR[0][(*r, rr)].astype(F32)).astype(BF16)
            else:
                W[(*h, rr)] = W[(*h, rr)] + FR[lvl][(*r, rr)].astype(F32)
        chunks((wsel if lvl else hsel)(p, lvl, grp, off), rsel(p, lvl, grp), body)
    def add_s(p, lvl, grp):
        rr = rows(FULL[p])
        def body(h, r):
            w = r if lvl == 0 else h
            own = H[(*h, rr)].astype(F32) if lvl == 0 else W[(*h, rr)]
            W[(*w, rr)] = own + SR[lvl][(0, *r, rr)].astype(F32) + SR[lvl][(1, *r, rr)].astype(F32)
        chunks((wsel if lvl else hsel)(p, lvl, grp, 0), rsel(p, lvl, grp), body)
    def middle(lvl, groups):
        for grp in groups:
            for p in range(3):
                tags["f", p, lvl, grp, 1].wait_recv()
                add_f(p, lvl, grp, 1)
                send_s(p, lvl, grp, 1, 0)
                tags["f", p, lvl, grp, 3].wait_recv()
                add_f(p, lvl, grp, 3)
                send_s(p, lvl, grp, 3, 1)
    def wait_s(p, lvl, grp):
        for off in (1, 3):
            for half in (0, 1):
                tags["s", p, lvl, grp, off, half].wait_recv()
    for grp in ORDER:
        for p in range(3):
            fill(p, grp, 2)
            send_f(p, 0, grp)
    for grp in ORDER:
        for p in range(3):
            fill(p, grp, 1)
            send_s(p, 0, grp, 1, 1)
            fill(p, grp, 3)
            send_s(p, 0, grp, 3, 0)
    middle(0, ORDER[:2])
    for grp in ORDER:
        for p in range(3):
            fill(p, grp, 0)
    middle(0, ORDER[2:])
    for grp in ORDER:
        for p in range(3):
            wait_s(p, 0, grp)
            add_s(p, 0, grp)
            for o1 in ORDER:
                if grp == 2:
                    send_f(p, 1, o1)
                elif grp == 1:
                    send_s(p, 1, o1, 1, 1)
                elif grp == 3:
                    send_s(p, 1, o1, 3, 0)
    middle(1, ORDER)
    for grp in ORDER:
        for p in range(3):
            wait_s(p, 1, grp)
            add_s(p, 1, grp)
            if grp == 2:
                send_f(p, 2, 0)
            elif grp == 1:
                send_s(p, 2, 0, 1, 1)
            elif grp == 3:
                send_s(p, 2, 0, 3, 0)
    middle(2, (0,))
    for p in range(3):
        wait_s(p, 2, 0)
    def finish():
        for c in pend:
            c.wait_send()
    assert count[0] == NR, count[0]
    def total(r0, r1):
        out = []
        for p in range(3):
            lo, hi = max(r0, FULL[p][0]), min(r1, FULL[p][1])
            if lo < hi:
                rr = pl.ds(lo, hi - lo)
                out.append(W[(*(pos[d] for d in sorted(DIMS[p][:2])), rr)] + SR[2][0, rr].astype(F32) + SR[2][1, rr].astype(F32))
        return jnp.concatenate(out, axis=0)
    return total, finish

NR = 162
def RS_SCRATCH(tb, tc):
    return [pltpu.VMEM((4, 4, 4, 640, 128), BF16), pltpu.VMEM((4, 4, 640, 128), F32),
    pltpu.VMEM((4, 4, 640, 128), BF16), pltpu.VMEM((4, 640, 128), tb), pltpu.VMEM((640, 128), tc),
    pltpu.VMEM((2, 4, 4, 640, 128), BF16), pltpu.VMEM((2, 4, 640, 128), tb), pltpu.VMEM((2, 640, 128), tc),
    pltpu.SemaphoreType.DMA((NR,)), pltpu.SemaphoreType.DMA((NR,))]

def parts_of(half):
    a = -(-half // 24) * 8
    return ((0, a), (a, 2 * a), (2 * a, half))

def all_reduce(M, T, RB, send, recv, pos, core):
    R = M.shape[0]; half = R // 2
    pend = []
    other = dev(pos, 1 - core)
    n = [0]
    def copy(src, dst, to):
        i = n[0]; n[0] += 1
        c = pltpu.make_async_remote_copy(src, dst, send.at[i], recv.at[i], device_id=to, device_id_type=MESH)
        c.start(); pend.append(c); return c
    mine = pl.ds(pl.multiple_of(core * half, 8), half)
    theirs = pl.ds(pl.multiple_of((1 - core) * half, 8), half)
    first = copy(M.at[theirs], T.at[4], other)
    first.wait_recv()
    T[0] = M[mine] + T[4]
    P = parts_of(half)
    got = {}
    def sends(p, k):
        d = DIMS[p][k]
        me = pos[d]
        rr = rows(P[p])
        RB[k, me, rr] = T[k, rr]
        for off in (2, 1, 3):
            got[p, k, off] = copy(T.at[k, rr], RB.at[k, me, rr], dev(moved(pos, d, off), core))
    for p in range(3):
        sends(p, 0)
    for k in range(3):
        for p in range(3):
            rr = rows(P[p])
            for off in (1, 3, 2):
                got[p, k, off].wait_recv()
            T[k + 1, rr] = (RB[k, 0, rr] + RB[k, 1, rr]) + (RB[k, 2, rr] + RB[k, 3, rr])
            if k < 2:
                sends(p, k + 1)
    c = copy(T.at[3], T.at[5], other)
    M[mine] = T[3]
    c.wait_recv()
    first.wait_send()
    M[theirs] = T[5]
    for c in pend[1:]:
        c.wait_send()
    assert n[0] == NG

NG = 29
def AR_SCRATCH(R):
    return [pltpu.VMEM((6, R // 2, 128), F32), pltpu.VMEM((3, 4, R // 2, 128), F32),
            pltpu.SemaphoreType.DMA((NG,)), pltpu.SemaphoreType.DMA((NG,))]

def gram(a, b):
    return lax.dot_general(a, b, (((0,), (0,)), ((), ())), precision=lax.Precision.HIGHEST, preferred_element_type=F32)

def rs_kernel(m, proj, tab, d_ref, prior, image, grams, H, W, FA, FB, FC, SA, SB, SC, send, recv, T, RB, gsend, grecv):
    pos, core = coords()
    barrier_all(pos, core, True)
    total, finish = reduce_scatter(proj, tab, H, W, (FA, FB, FC), (SA, SB, SC), send, recv, pos, core)
    for b in range(5):
        rr = pl.ds(b * 128, 128)
        image[rr] = prior[rr] * d_ref[rr] + total(b * 128, b * 128 + 128).T
    grams[pl.ds(0, 128)] = gram(d_ref[...], image[...])
    if m > 1:
        grams[pl.ds(128, 128)] = gram(image[...], image[...])
        grams[pl.ds(256, 128)] = gram(d_ref[...], d_ref[...])
    all_reduce(grams, T, RB, gsend, grecv, pos, core)
    finish()

def rs_call(m, proj, tab, d, prior):
    V = pl.BlockSpec(memory_space=pltpu.VMEM)
    return pl.pallas_call(functools.partial(rs_kernel, m),
        out_shape=(jax.ShapeDtypeStruct((640, 128), F32), jax.ShapeDtypeStruct((128 * m, 128), F32)),
        in_specs=[V, pl.BlockSpec(memory_space=pltpu.SMEM), V, V], out_specs=(V, V),
        scratch_shapes=RS_SCRATCH(F32, F32) + AR_SCRATCH(128 * m),
        compiler_params=pltpu.CompilerParams(collective_id=1 + m, has_side_effects=True, vmem_limit_bytes=40 << 20),
    )(proj, tab, d, prior)

F32, BF16 = jnp.float32, jnp.bfloat16
def nt(a, b):
    return lax.dot_general(a, b, (((1,), (1,)), ((), ())), preferred_element_type=F32).astype(BF16)
def nn(a, b):
    return lax.dot_general(a, b, (((1,), (0,)), ((), ())), preferred_element_type=F32).astype(BF16)

def k1_kernel(v_ref, idx_ref, panel_h, fac_h, proj, G, panel, fac, send, recv, csend, crecv, lsem, psend, precv):
    pos, core = coords()
    lp = pltpu.make_async_copy(panel_h, panel, lsem.at[0])
    lf = pltpu.make_async_copy(fac_h, fac, lsem.at[1])
    for b in range(5):
        G[pos[0], pos[1], pos[2], core, pl.ds(b * 128, 128)] = v_ref[pl.ds(b * 128, 128)].T.astype(BF16)
    entry_barrier(pos, core)
    lp.start(); lf.start()
    n = gather_all(G, send, recv, csend, crecv, pos, core)
    assert n == (NS, NC), n
    proj[256] = jnp.zeros((128, 128), BF16)
    lp.wait(); lf.wait()
    copies = lambda a: pltpu.make_async_remote_copy(proj.at[pl.ds(a * 8, 8)], proj.at[pl.ds(128 + a * 8, 8)],
        psend.at[a], precv.at[a], device_id=dev(pos, 1 - core), device_id_type=MESH)
    blocks = G.reshape(640, 128, 128)
    def arc(a, _):
        cat = []
        for k in range(8):
            cat.append(blocks[idx_ref[a * 8 + k]])
        x = jnp.concatenate(cat, axis=1)
        f = fac[a]
        s = nn(nt(nt(x, panel[a]), f), f)
        y = nn(s, panel[a])
        for k in range(8):
            proj[a * 8 + k] = y[:, k * 128:(k + 1) * 128]
        copies(a).start()
        return 0
    lax.fori_loop(0, 16, arc, 0)
    def fin(a, _):
        copies(a).wait()
        return 0
    lax.fori_loop(0, 16, fin, 0)

def k1_call(v, idx, panel, fac):
    V = pl.BlockSpec(memory_space=pltpu.VMEM); A = pl.BlockSpec(memory_space=pl.ANY)
    return pl.pallas_call(k1_kernel,
        out_shape=jax.ShapeDtypeStruct((257, 128, 128), BF16),
        in_specs=[V, pl.BlockSpec(memory_space=pltpu.SMEM), A, A], out_specs=V,
        scratch_shapes=[pltpu.VMEM((4, 4, 4, 2, 640, 128), BF16), pltpu.VMEM((16, 256, 1024), BF16), pltpu.VMEM((16, 256, 256), BF16),
            pltpu.SemaphoreType.DMA((NS,)), pltpu.SemaphoreType.DMA((NS,)),
            pltpu.SemaphoreType.DMA((NC,)), pltpu.SemaphoreType.DMA((NC,)), pltpu.SemaphoreType.DMA((2,)),
            pltpu.SemaphoreType.DMA((16,)), pltpu.SemaphoreType.DMA((16,))],
        compiler_params=pltpu.CompilerParams(collective_id=0, has_side_effects=True, vmem_limit_bytes=45 << 20),
    )(v, idx, panel, fac)

HI = lax.Precision.HIGHEST
def mm(a, b): return jnp.dot(a, b, precision=HI)
def tables(owner, block, me, core):
    g = owner * 5 + block
    mine = lax.dynamic_slice_in_dim(g.reshape(128, 128), me, 1, 0).reshape(128)
    theirs = lax.dynamic_slice_in_dim(g.reshape(128, 128), me + 1 - 2 * core, 1, 0).reshape(128)
    def two(row, base):
        e = jnp.arange(128, dtype=jnp.int32)
        hit = row[None, :] == jnp.arange(640, dtype=jnp.int32)[:, None]
        first = jnp.min(jnp.where(hit, e[None], 999), axis=1)
        last = jnp.max(jnp.where(hit, e[None], -1), axis=1)
        return jnp.where(first < 999, first + base, 256), jnp.where(last > first, last + base, 256)
    t = jnp.stack([*two(mine, 0), *two(theirs, 128)], axis=1).reshape(-1).astype(jnp.int32)
    return mine, t
def solve(a, b):
    return jax.scipy.linalg.cho_solve((jnp.linalg.cholesky(a), True), b)
def per_device(right_side, prior_diag, inv_factor, coupling_panel, owner, block):
    me = lax.axis_index(("arc", "vec"))
    core = me % 2
    idx, tab = tables(owner, block, me, core)
    b = right_side.reshape(640, 128)
    prior = jnp.broadcast_to(prior_diag.reshape(640, 1), (640, 128))
    proj = k1_call(b, idx, coupling_panel, inv_factor)
    image, grams = rs_call(3, proj, tab, b, prior)
    c, g2, g0 = grams[:128], grams[128:256], grams[256:]
    alpha = solve(c, g0)
    ca = mm(c, alpha)
    new = g0 - ca - ca.T + mm(alpha.T, mm(g2, alpha))
    beta = solve(g0, new)
    x = mm(b, alpha)
    r = b - mm(image, alpha)
    d = r + mm(b, beta)
    proj = k1_call(d, idx, coupling_panel, inv_factor)
    image, c = rs_call(1, proj, tab, d, prior)
    alpha = solve(c, new)
    x = x + mm(d, alpha)
    r = r - mm(image, alpha)
    return x.reshape(5, 128, 128), r.reshape(5, 128, 128)
def solution(mesh):
    ins = (P(("arc", "vec"), None, None), P(("arc", "vec"), None), P(("arc", "vec"), None, None), P(("arc", "vec"), None, None), P(), P())
    outs = (P(("arc", "vec"), None, None), P(("arc", "vec"), None, None))
    return jax.shard_map(per_device, mesh=mesh, in_specs=ins, out_specs=outs, check_vma=False)
```

```python
import functools
import jax
import jax.numpy as jnp
from jax import lax
from jax.experimental import pallas as pl
from jax.experimental.pallas import tpu as pltpu
from jax.sharding import PartitionSpec as P
MESH = pl.DeviceIdType.MESH
DIMS = ((0, 1, 2), (1, 2, 0), (2, 0, 1))
CUT = ((0, 112, 208), (208, 320, 432), (432, 528, 640))
OFFS = (0, 3, 1, 2)

def coords():
    arc, vec = lax.axis_index("arc"), lax.axis_index("vec")
    return (arc // 4, arc % 4, vec // 2), vec % 2

def dev(pos, core):
    return (pos[0] * 4 + pos[1], pos[2] * 2 + core)

def moved(pos, dim, off):
    return tuple((p + off) % 4 if d == dim else p for d, p in enumerate(pos))

def entry_barrier(pos, core):
    barrier = pltpu.get_barrier_semaphore()
    for dim in range(3):
        for off in (1, 3):
            pl.semaphore_signal(barrier, inc=1, device_id=dev(moved(pos, dim, off), core), device_id_type=MESH)
    pl.semaphore_signal(barrier, inc=1, device_id=dev(pos, 1 - core), device_id_type=MESH)
    pl.semaphore_wait(barrier, 7)

def gather_all(G, send, recv, csend, crecv, pos, core):
    pend = []
    cpend = []
    nsem = [0]
    ncs = [0]
    def at(sel, cc, rows):
        return G.at[sel[0], sel[1], sel[2], cc, pl.ds(rows[0], rows[1] - rows[0])]
    def make(sel_src, dim, off, rows):
        i = nsem[0]; nsem[0] += 1
        ref = at(sel_src, core, rows)
        return pltpu.make_async_remote_copy(ref, ref, send.at[i], recv.at[i],
            device_id=dev(moved(pos, dim, off), core), device_id_type=MESH)
    def start(sel, dim, off, rows):
        c = make(sel, dim, off, rows); c.start(); pend.append(c); return c
    def cross(sel, rows):
        i = ncs[0]; ncs[0] += 1
        ref = at(sel, core, rows)
        c = pltpu.make_async_remote_copy(ref, ref, csend.at[i], crecv.at[i],
            device_id=dev(pos, 1 - core), device_id_type=MESH)
        c.start(); cpend.append(c)
    def rel(dim, off):
        return moved(pos, dim, off)
    def allof(sel, *dims):
        return tuple(slice(None) if d in dims else s for d, s in enumerate(sel))
    A = [(c[0], c[1]) for c in CUT]; B = [(c[1], c[2]) for c in CUT]; F = [(c[0], c[2]) for c in CUT]
    s1 = {}; f1 = {}; s2 = {}; f2 = {}; s3 = {}; f3 = {}
    def S2(p, o1):
        d1, d2, d3 = DIMS[p]
        for off in (1, 3):
            s2[p, o1, off] = start(moved(pos, d1, o1), d2, off, F[p])
    def S3(p, o2):
        d1, d2, d3 = DIMS[p]
        for off in (1, 3):
            s3[p, o2, off] = start(allof(moved(pos, d2, o2), d1), d3, off, F[p])
    for p in range(3):
        d1 = DIMS[p][0]
        for off in (1, 3):
            s1[p, off] = start(pos, d1, off, F[p])
    for p in range(3):
        S2(p, 0)
    cross(pos, (0, 640))
    for p in range(3):
        d1 = DIMS[p][0]
        s1[p, 1].wait_recv()
        f1[p, 1] = start(rel(d1, 3), d1, 1, A[p])
        s1[p, 3].wait_recv()
        f1[p, 3] = start(rel(d1, 1), d1, 3, B[p])
    for p in range(3):
        S2(p, 3); S2(p, 1)
        d1 = DIMS[p][0]
        cross(rel(d1, 3), F[p]); cross(rel(d1, 1), F[p])
    for p in range(3):
        f1[p, 1].wait_recv(); f1[p, 3].wait_recv()
        S2(p, 2)
        S3(p, 0)
        cross(rel(DIMS[p][0], 2), F[p])
    for o1 in OFFS:
        for p in range(3):
            d1, d2, d3 = DIMS[p]
            s2[p, o1, 1].wait_recv()
            f2[p, o1, 1] = start(moved(rel(d1, o1), d2, 3), d2, 1, A[p])
            s2[p, o1, 3].wait_recv()
            f2[p, o1, 3] = start(moved(rel(d1, o1), d2, 1), d2, 3, B[p])
    for p in range(3):
        d1, d2, d3 = DIMS[p]
        S3(p, 3); S3(p, 1)
        cross(allof(rel(d2, 3), d1), F[p]); cross(allof(rel(d2, 1), d1), F[p])
    for p in range(3):
        d1, d2, d3 = DIMS[p]
        for o1 in OFFS:
            f2[p, o1, 1].wait_recv(); f2[p, o1, 3].wait_recv()
        S3(p, 2)
        cross(allof(rel(d2, 2), d1), F[p])
    for o2 in OFFS:
        for p in range(3):
            d1, d2, d3 = DIMS[p]
            s3[p, o2, 1].wait_recv()
            sel = allof(moved(rel(d2, o2), d3, 3), d1)
            f3[p, o2, 1] = start(sel, d3, 1, A[p])
            cross(sel, F[p])
            s3[p, o2, 3].wait_recv()
            sel = allof(moved(rel(d2, o2), d3, 1), d1)
            f3[p, o2, 3] = start(sel, d3, 3, B[p])
            cross(sel, F[p])
    for o2 in OFFS:
        for p in range(3):
            d1, d2, d3 = DIMS[p]
            f3[p, o2, 1].wait_recv(); f3[p, o2, 3].wait_recv()
            cross(allof(moved(rel(d2, o2), d3, 2), d1), F[p])
    for c in cpend:
        c.wait_recv()
    for c in pend + cpend:
        c.wait_send()
    return nsem[0], ncs[0]

NS, NC = 108, 55


ORDER = (2, 1, 3, 0)
F32, BF16 = jnp.float32, jnp.bfloat16
FULL = [(c[0], c[2]) for c in CUT]; HA = [(c[0], c[1]) for c in CUT]; HB = [(c[1], c[2]) for c in CUT]

def barrier_all(pos, core, far):
    barrier = pltpu.get_barrier_semaphore()
    offs = (1, 2, 3) if far else (1, 3)
    for dim in range(3):
        for off in offs:
            pl.semaphore_signal(barrier, inc=1, device_id=dev(moved(pos, dim, off), core), device_id_type=MESH)
    pl.semaphore_signal(barrier, inc=1, device_id=dev(pos, 1 - core), device_id_type=MESH)
    pl.semaphore_wait(barrier, 3 * len(offs) + 1)

def pieces(p):
    lo, hi = FULL[p]
    out = []
    for b in range(5):
        r0, r1 = max(lo, b * 128), min(hi, b * 128 + 128)
        if r0 < r1:
            out.append((b, r0 - b * 128, r1 - b * 128))
    return out

def rows(r):
    return pl.ds(r[0], r[1] - r[0])

def reduce_scatter(proj, tab, H, W, FR, SR, send, recv, pos, core):
    count = [0]
    pend = []
    tags = {}
    def ring_dim(p, lvl):
        return DIMS[p][2 - lvl]
    def hsel(p, lvl, grp, off):
        d1, d2, d3 = DIMS[p]
        sel = list(pos)
        if lvl == 0:
            sel[d1] = slice(None); sel[d2] = (pos[d2] + grp) % 4; sel[d3] = (pos[d3] + off) % 4
        elif lvl == 1:
            sel[d1] = (pos[d1] + grp) % 4; sel[d2] = (pos[d2] + off) % 4
        else:
            sel[d1] = (pos[d1] + off) % 4
        return tuple(sel)
    def rsel(p, lvl, grp):
        d1, d2, d3 = DIMS[p]
        if lvl == 0:
            return tuple(slice(None) if d == d1 else (pos[d2] + grp) % 4 for d in sorted((d1, d2)))
        if lvl == 1:
            return ((pos[d1] + grp) % 4,)
        return ()
    def wsel(p, lvl, grp, off):
        h = hsel(p, lvl, grp, off)
        return tuple(h[d] for d in sorted(DIMS[p][:2]))
    def source(p, lvl, grp, off, rr):
        if lvl == 0:
            return H.at[(*hsel(p, lvl, grp, off), rows(rr))]
        return W.at[(*wsel(p, lvl, grp, off), rows(rr))]
    def start(src, dst, p, lvl, off, tag):
        i = count[0]; count[0] += 1
        c = pltpu.make_async_remote_copy(src, dst, send.at[i], recv.at[i],
            device_id=dev(moved(pos, ring_dim(p, lvl), off), core), device_id_type=MESH)
        c.start(); pend.append(c); tags[tag] = c
    def send_f(p, lvl, grp):
        r = rsel(p, lvl, grp)
        start(source(p, lvl, grp, 2, HA[p]), FR[lvl].at[(*r, rows(HA[p]))], p, lvl, 1, ("f", p, lvl, grp, 1))
        start(source(p, lvl, grp, 2, HB[p]), FR[lvl].at[(*r, rows(HB[p]))], p, lvl, 3, ("f", p, lvl, grp, 3))
    def send_s(p, lvl, grp, off, half):
        r = rsel(p, lvl, grp)
        rr = (HA if half == 0 else HB)[p]
        start(source(p, lvl, grp, off, rr), SR[lvl].at[(0 if off == 1 else 1, *r, rows(rr))], p, lvl, off, ("s", p, lvl, grp, off, half))
    def chunks(h, r, body):
        if any(isinstance(s, slice) for s in h):
            def step(i, _):
                body(tuple(i if isinstance(s, slice) else s for s in h), tuple(i if isinstance(s, slice) else s for s in r))
                return 0
            lax.fori_loop(0, 4, step, 0)
        else:
            body(h, r)
    def fill(p, grp, off):
        def body(h, r):
            g0 = ((h[0] * 4 + h[1]) * 8 + h[2] * 2 + core) * 5
            for b, r0, r1 in pieces(p):
                rr = pl.ds(r0, r1 - r0)
                e = [tab[(g0 + b) * 4 + k] for k in range(4)]
                v = (proj[e[0], rr] + proj[e[1], rr]) + (proj[e[2], rr] + proj[e[3], rr])
                H[(*h, pl.ds(b * 128 + r0, r1 - r0))] = v
        h = hsel(p, 0, grp, off)
        chunks(h, h, body)
    def add_f(p, lvl, grp, off):
        rr = rows((HA if off == 1 else HB)[p])
        def body(h, r):
            if lvl == 0:
                H[(*h, rr)] = (H[(*h, rr)].astype(F32) + FR[0][(*r, rr)].astype(F32)).astype(BF16)
            else:
                W[(*h, rr)] = W[(*h, rr)] + FR[lvl][(*r, rr)].astype(F32)
        chunks((wsel if lvl else hsel)(p, lvl, grp, off), rsel(p, lvl, grp), body)
    def add_s(p, lvl, grp):
        rr = rows(FULL[p])
        def body(h, r):
            w = r if lvl == 0 else h
            own = H[(*h, rr)].astype(F32) if lvl == 0 else W[(*h, rr)]
            W[(*w, rr)] = own + SR[lvl][(0, *r, rr)].astype(F32) + SR[lvl][(1, *r, rr)].astype(F32)
        chunks((wsel if lvl else hsel)(p, lvl, grp, 0), rsel(p, lvl, grp), body)
    def middle(lvl, groups):
        for grp in groups:
            for p in range(3):
                tags["f", p, lvl, grp, 1].wait_recv()
                add_f(p, lvl, grp, 1)
                send_s(p, lvl, grp, 1, 0)
                tags["f", p, lvl, grp, 3].wait_recv()
                add_f(p, lvl, grp, 3)
                send_s(p, lvl, grp, 3, 1)
    def wait_s(p, lvl, grp):
        for off in (1, 3):
            for half in (0, 1):
                tags["s", p, lvl, grp, off, half].wait_recv()
    for grp in ORDER:
        for p in range(3):
            fill(p, grp, 2)
            send_f(p, 0, grp)
    for grp in ORDER:
        for p in range(3):
            fill(p, grp, 1)
            send_s(p, 0, grp, 1, 1)
            fill(p, grp, 3)
            send_s(p, 0, grp, 3, 0)
    middle(0, ORDER[:2])
    for grp in ORDER:
        for p in range(3):
            fill(p, grp, 0)
    middle(0, ORDER[2:])
    for grp in ORDER:
        for p in range(3):
            wait_s(p, 0, grp)
            add_s(p, 0, grp)
            for o1 in ORDER:
                if grp == 2:
                    send_f(p, 1, o1)
                elif grp == 1:
                    send_s(p, 1, o1, 1, 1)
                elif grp == 3:
                    send_s(p, 1, o1, 3, 0)
    middle(1, ORDER)
    for grp in ORDER:
        for p in range(3):
            wait_s(p, 1, grp)
            add_s(p, 1, grp)
            if grp == 2:
                send_f(p, 2, 0)
            elif grp == 1:
                send_s(p, 2, 0, 1, 1)
            elif grp == 3:
                send_s(p, 2, 0, 3, 0)
    middle(2, (0,))
    for p in range(3):
        wait_s(p, 2, 0)
    def finish():
        for c in pend:
            c.wait_send()
    assert count[0] == NR, count[0]
    def total(r0, r1):
        out = []
        for p in range(3):
            lo, hi = max(r0, FULL[p][0]), min(r1, FULL[p][1])
            if lo < hi:
                rr = pl.ds(lo, hi - lo)
                out.append(W[(*(pos[d] for d in sorted(DIMS[p][:2])), rr)] + SR[2][0, rr].astype(F32) + SR[2][1, rr].astype(F32))
        return jnp.concatenate(out, axis=0)
    return total, finish

NR = 162
def RS_SCRATCH(tb, tc):
    return [pltpu.VMEM((4, 4, 4, 640, 128), BF16), pltpu.VMEM((4, 4, 640, 128), F32),
    pltpu.VMEM((4, 4, 640, 128), BF16), pltpu.VMEM((4, 640, 128), tb), pltpu.VMEM((640, 128), tc),
    pltpu.VMEM((2, 4, 4, 640, 128), BF16), pltpu.VMEM((2, 4, 640, 128), tb), pltpu.VMEM((2, 640, 128), tc),
    pltpu.SemaphoreType.DMA((NR,)), pltpu.SemaphoreType.DMA((NR,))]

def parts_of(half):
    a = -(-half // 24) * 8
    return ((0, a), (a, 2 * a), (2 * a, half))

def all_reduce(M, T, RB, send, recv, pos, core):
    R = M.shape[0]; half = R // 2
    pend = []
    other = dev(pos, 1 - core)
    n = [0]
    def copy(src, dst, to):
        i = n[0]; n[0] += 1
        c = pltpu.make_async_remote_copy(src, dst, send.at[i], recv.at[i], device_id=to, device_id_type=MESH)
        c.start(); pend.append(c); return c
    mine = pl.ds(pl.multiple_of(core * half, 8), half)
    theirs = pl.ds(pl.multiple_of((1 - core) * half, 8), half)
    first = copy(M.at[theirs], T.at[4], other)
    first.wait_recv()
    T[0] = M[mine] + T[4]
    P = parts_of(half)
    got = {}
    def sends(p, k):
        d = DIMS[p][k]
        me = pos[d]
        rr = rows(P[p])
        RB[k, me, rr] = T[k, rr]
        for off in (2, 1, 3):
            got[p, k, off] = copy(T.at[k, rr], RB.at[k, me, rr], dev(moved(pos, d, off), core))
    for p in range(3):
        sends(p, 0)
    for k in range(3):
        for p in range(3):
            rr = rows(P[p])
            for off in (1, 3, 2):
                got[p, k, off].wait_recv()
            T[k + 1, rr] = (RB[k, 0, rr] + RB[k, 1, rr]) + (RB[k, 2, rr] + RB[k, 3, rr])
            if k < 2:
                sends(p, k + 1)
    c = copy(T.at[3], T.at[5], other)
    M[mine] = T[3]
    c.wait_recv()
    first.wait_send()
    M[theirs] = T[5]
    for c in pend[1:]:
        c.wait_send()
    assert n[0] == NG

NG = 29
def AR_SCRATCH(R):
    return [pltpu.VMEM((6, R // 2, 128), F32), pltpu.VMEM((3, 4, R // 2, 128), F32),
            pltpu.SemaphoreType.DMA((NG,)), pltpu.SemaphoreType.DMA((NG,))]

def gram(a, b):
    return lax.dot_general(a, b, (((0,), (0,)), ((), ())), precision=lax.Precision.HIGHEST, preferred_element_type=F32)

def rs_kernel(m, proj, tab, d_ref, prior, image, grams, H, W, FA, FB, FC, SA, SB, SC, send, recv, T, RB, gsend, grecv):
    pos, core = coords()
    barrier_all(pos, core, True)
    total, finish = reduce_scatter(proj, tab, H, W, (FA, FB, FC), (SA, SB, SC), send, recv, pos, core)
    for b in range(5):
        rr = pl.ds(b * 128, 128)
        image[rr] = prior[rr] * d_ref[rr] + total(b * 128, b * 128 + 128).T
    grams[pl.ds(0, 128)] = gram(d_ref[...], image[...])
    if m > 1:
        grams[pl.ds(128, 128)] = gram(image[...], image[...])
        grams[pl.ds(256, 128)] = gram(d_ref[...], d_ref[...])
    all_reduce(grams, T, RB, gsend, grecv, pos, core)
    finish()

def rs_call(m, proj, tab, d, prior):
    V = pl.BlockSpec(memory_space=pltpu.VMEM)
    return pl.pallas_call(functools.partial(rs_kernel, m),
        out_shape=(jax.ShapeDtypeStruct((640, 128), F32), jax.ShapeDtypeStruct((128 * m, 128), F32)),
        in_specs=[V, pl.BlockSpec(memory_space=pltpu.SMEM), V, V], out_specs=(V, V),
        scratch_shapes=RS_SCRATCH(F32, F32) + AR_SCRATCH(128 * m),
        compiler_params=pltpu.CompilerParams(collective_id=1 + m, has_side_effects=True, vmem_limit_bytes=34 << 20),
    )(proj, tab, d, prior)

F32, BF16 = jnp.float32, jnp.bfloat16
def nt(a, b):
    return lax.dot_general(a, b, (((1,), (1,)), ((), ())), preferred_element_type=F32).astype(BF16)
def nn(a, b):
    return lax.dot_general(a, b, (((1,), (0,)), ((), ())), preferred_element_type=F32).astype(BF16)

def k1_kernel(v_ref, idx_ref, panel_h, fac_h, proj, G, panel, fac, send, recv, csend, crecv, lsem, psend, precv):
    pos, core = coords()
    lp = pltpu.make_async_copy(panel_h, panel, lsem.at[0])
    lf = pltpu.make_async_copy(fac_h, fac, lsem.at[1])
    for b in range(5):
        G[pos[0], pos[1], pos[2], core, pl.ds(b * 128, 128)] = v_ref[pl.ds(b * 128, 128)].T.astype(BF16)
    entry_barrier(pos, core)
    lp.start(); lf.start()
    n = gather_all(G, send, recv, csend, crecv, pos, core)
    assert n == (NS, NC), n
    proj[256] = jnp.zeros((128, 128), BF16)
    lp.wait(); lf.wait()
    copies = lambda a: pltpu.make_async_remote_copy(proj.at[pl.ds(a * 8, 8)], proj.at[pl.ds(128 + a * 8, 8)],
        psend.at[a], precv.at[a], device_id=dev(pos, 1 - core), device_id_type=MESH)
    blocks = G.reshape(640, 128, 128)
    def arc(a, _):
        cat = []
        for k in range(8):
            cat.append(blocks[idx_ref[a * 8 + k]])
        x = jnp.concatenate(cat, axis=1)
        f = fac[a]
        s = nn(nt(nt(x, panel[a]), f), f)
        y = nn(s, panel[a])
        for k in range(8):
            proj[a * 8 + k] = y[:, k * 128:(k + 1) * 128]
        copies(a).start()
        return 0
    lax.fori_loop(0, 16, arc, 0)
    def fin(a, _):
        copies(a).wait()
        return 0
    lax.fori_loop(0, 16, fin, 0)

def k1_call(v, idx, panel, fac):
    V = pl.BlockSpec(memory_space=pltpu.VMEM); A = pl.BlockSpec(memory_space=pltpu.HBM)
    return pl.pallas_call(k1_kernel,
        out_shape=jax.ShapeDtypeStruct((257, 128, 128), BF16),
        in_specs=[V, pl.BlockSpec(memory_space=pltpu.SMEM), A, A], out_specs=V,
        scratch_shapes=[pltpu.VMEM((4, 4, 4, 2, 640, 128), BF16), pltpu.VMEM((16, 256, 1024), BF16), pltpu.VMEM((16, 256, 256), BF16),
            pltpu.SemaphoreType.DMA((NS,)), pltpu.SemaphoreType.DMA((NS,)),
            pltpu.SemaphoreType.DMA((NC,)), pltpu.SemaphoreType.DMA((NC,)), pltpu.SemaphoreType.DMA((2,)),
            pltpu.SemaphoreType.DMA((16,)), pltpu.SemaphoreType.DMA((16,))],
        compiler_params=pltpu.CompilerParams(collective_id=0, has_side_effects=True, vmem_limit_bytes=33 << 20),
    )(v, idx, panel, fac)

F32 = jnp.float32
def hdot(a, b, ca=1):
    return lax.dot_general(a, b, (((ca,), (0,)), ((), ())), precision=lax.Precision.HIGHEST, preferred_element_type=F32)

def negated_inverses(mats):
    lane = lax.broadcasted_iota(jnp.int32, (8, 128), 1)
    sub = lax.broadcasted_iota(jnp.int32, (8, 128), 0)
    wide = lax.broadcasted_iota(jnp.int32, (128, 128), 1)
    def sweep(_, carry):
        out = []
        tops = [a[:8] for a in carry]
        ws = list(tops)
        for j in range(0, 8, 2):
            for m in range(len(ws)):
                w = ws[m]
                col0 = jnp.broadcast_to(w[:, j:j + 1], (8, 128))
                col1 = jnp.broadcast_to(w[:, j + 1:j + 2], (8, 128))
                row0 = jnp.where(lane == j, 1.0, jnp.where(lane == j + 1, 0.0, jnp.broadcast_to(w[j:j + 1, :], (8, 128))))
                row1 = jnp.where(lane == j + 1, 1.0, jnp.where(lane == j, 0.0, jnp.broadcast_to(w[j + 1:j + 2, :], (8, 128))))
                a00 = jnp.broadcast_to(col0[j:j + 1, :], (8, 128))
                a10 = jnp.broadcast_to(col0[j + 1:j + 2, :], (8, 128))
                a01 = jnp.broadcast_to(col1[j:j + 1, :], (8, 128))
                a11 = jnp.broadcast_to(col1[j + 1:j + 2, :], (8, 128))
                inv = 1.0 / (a00 * a11 - a01 * a10)
                new0 = (a11 * row0 - a01 * row1) * inv
                new1 = (a00 * row1 - a10 * row0) * inv
                w = jnp.where((lane == j) | (lane == j + 1), 0.0, w) - col0 * new0 - col1 * new1
                ws[m] = jnp.where(sub == j, new0, jnp.where(sub == j + 1, new1, w))
        for a, p, w in zip(carry, tops, ws):
            m = hdot(jnp.where(lane < 8, 0.0, p), w, 0)
            rest = jnp.where(wide < 8, m, a - m)
            first = jnp.where(lane < 8, -w, w)
            out.append(pltpu.roll(jnp.concatenate([rest[8:], first], axis=0), 120, 1))
        return tuple(out)
    return lax.fori_loop(0, 16, sweep, tuple(mats))

def sym(a):
    return (a + a.T) * 0.5

def first_kernel(grams, b, image, x, r, d, new):
    c, g2, g0 = grams[pl.ds(0, 128)], grams[pl.ds(128, 128)], grams[pl.ds(256, 128)]
    ci, gi = negated_inverses((sym(c), sym(g0)))
    alpha = -hdot(ci, g0)
    ca = hdot(c, alpha)
    ng = g0 - ca - ca.T + hdot(alpha, hdot(g2, alpha), 0)
    beta = -hdot(gi, ng)
    new[...] = ng
    bb = b[...]
    x[...] = hdot(bb, alpha)
    rr = bb - hdot(image[...], alpha)
    r[...] = rr
    d[...] = rr + hdot(bb, beta)

def last_kernel(c, new, x0, r0, d, image, x, r):
    (ci,) = negated_inverses((sym(c[...]),))
    alpha = -hdot(ci, new[...])
    x[...] = x0[...] + hdot(d[...], alpha)
    r[...] = r0[...] - hdot(image[...], alpha)

def first_call(grams, b, image):
    big, small = jax.ShapeDtypeStruct((640, 128), F32), jax.ShapeDtypeStruct((128, 128), F32)
    V = pl.BlockSpec(memory_space=pltpu.VMEM)
    return pl.pallas_call(first_kernel, out_shape=(big, big, big, small), in_specs=[V] * 3, out_specs=(V,) * 4,
        compiler_params=pltpu.CompilerParams(vmem_limit_bytes=16 << 20))(grams, b, image)

def last_call(c, new, x0, r0, d, image):
    big = jax.ShapeDtypeStruct((640, 128), F32)
    V = pl.BlockSpec(memory_space=pltpu.VMEM)
    return pl.pallas_call(last_kernel, out_shape=(big, big), in_specs=[V] * 6, out_specs=(V,) * 2,
        compiler_params=pltpu.CompilerParams(vmem_limit_bytes=16 << 20))(c, new, x0, r0, d, image)

def tables(owner, block, me, core):
    g = owner * 5 + block
    mine = lax.dynamic_slice_in_dim(g.reshape(128, 128), me, 1, 0).reshape(128)
    theirs = lax.dynamic_slice_in_dim(g.reshape(128, 128), me + 1 - 2 * core, 1, 0).reshape(128)
    def two(row, base):
        e = jnp.arange(128, dtype=jnp.int32)
        hit = row[None, :] == jnp.arange(640, dtype=jnp.int32)[:, None]
        first = jnp.min(jnp.where(hit, e[None], 999), axis=1)
        last = jnp.max(jnp.where(hit, e[None], -1), axis=1)
        return jnp.where(first < 999, first + base, 256), jnp.where(last > first, last + base, 256)
    t = jnp.stack([*two(mine, 0), *two(theirs, 128)], axis=1).reshape(-1).astype(jnp.int32)
    return mine, t
def per_device(right_side, prior_diag, inv_factor, coupling_panel, owner, block):
    me = lax.axis_index(("arc", "vec"))
    core = me % 2
    idx, tab = tables(owner, block, me, core)
    b = right_side.reshape(640, 128)
    prior = jnp.broadcast_to(prior_diag.reshape(640, 1), (640, 128))
    proj = k1_call(b, idx, coupling_panel, inv_factor)
    image, grams = rs_call(3, proj, tab, b, prior)
    x, r, d, new = first_call(grams, b, image)
    proj = k1_call(d, idx, coupling_panel, inv_factor)
    image, c = rs_call(1, proj, tab, d, prior)
    x, r = last_call(c, new, x, r, d, image)
    return x.reshape(5, 128, 128), r.reshape(5, 128, 128)
def solution(mesh):
    ins = (P(("arc", "vec"), None, None), P(("arc", "vec"), None), P(("arc", "vec"), None, None), P(("arc", "vec"), None, None), P(), P())
    outs = (P(("arc", "vec"), None, None), P(("arc", "vec"), None, None))
    return jax.shard_map(per_device, mesh=mesh, in_specs=ins, out_specs=outs, check_vma=False)
```

```python
import functools
import jax
import jax.numpy as jnp
from jax import lax
from jax.experimental import pallas as pl
from jax.experimental.pallas import tpu as pltpu
from jax.sharding import PartitionSpec as P
MESH = pl.DeviceIdType.MESH
DIMS = ((0, 1, 2), (1, 2, 0), (2, 0, 1))
CUT = ((0, 112, 208), (208, 320, 432), (432, 528, 640))
OFFS = (0, 3, 1, 2)

def coords():
    arc, vec = lax.axis_index("arc"), lax.axis_index("vec")
    return (arc // 4, arc % 4, vec // 2), vec % 2

def dev(pos, core):
    return (pos[0] * 4 + pos[1], pos[2] * 2 + core)

def moved(pos, dim, off):
    return tuple((p + off) % 4 if d == dim else p for d, p in enumerate(pos))

def entry_barrier(pos, core):
    barrier = pltpu.get_barrier_semaphore()
    for dim in range(3):
        for off in (1, 3):
            pl.semaphore_signal(barrier, inc=1, device_id=dev(moved(pos, dim, off), core), device_id_type=MESH)
    pl.semaphore_signal(barrier, inc=1, device_id=dev(pos, 1 - core), device_id_type=MESH)
    pl.semaphore_wait(barrier, 7)

def gather_all(G, send, recv, csend, crecv, pos, core):
    pend = []
    cpend = []
    nsem = [0]
    ncs = [0]
    def at(sel, cc, rows):
        return G.at[sel[0], sel[1], sel[2], cc, pl.ds(rows[0], rows[1] - rows[0])]
    def make(sel_src, dim, off, rows):
        i = nsem[0]; nsem[0] += 1
        ref = at(sel_src, core, rows)
        return pltpu.make_async_remote_copy(ref, ref, send.at[i], recv.at[i],
            device_id=dev(moved(pos, dim, off), core), device_id_type=MESH)
    def start(sel, dim, off, rows):
        c = make(sel, dim, off, rows); c.start(); pend.append(c); return c
    def cross(sel, rows):
        i = ncs[0]; ncs[0] += 1
        ref = at(sel, core, rows)
        c = pltpu.make_async_remote_copy(ref, ref, csend.at[i], crecv.at[i],
            device_id=dev(pos, 1 - core), device_id_type=MESH)
        c.start(); cpend.append(c)
    def rel(dim, off):
        return moved(pos, dim, off)
    def allof(sel, *dims):
        return tuple(slice(None) if d in dims else s for d, s in enumerate(sel))
    A = [(c[0], c[1]) for c in CUT]; B = [(c[1], c[2]) for c in CUT]; F = [(c[0], c[2]) for c in CUT]
    s1 = {}; f1 = {}; s2 = {}; f2 = {}; s3 = {}; f3 = {}
    def S2(p, o1):
        d1, d2, d3 = DIMS[p]
        for off in (1, 3):
            s2[p, o1, off] = start(moved(pos, d1, o1), d2, off, F[p])
    def S3(p, o2):
        d1, d2, d3 = DIMS[p]
        for off in (1, 3):
            s3[p, o2, off] = start(allof(moved(pos, d2, o2), d1), d3, off, F[p])
    for p in range(3):
        d1 = DIMS[p][0]
        for off in (1, 3):
            s1[p, off] = start(pos, d1, off, F[p])
    for p in range(3):
        S2(p, 0)
    cross(pos, (0, 640))
    for p in range(3):
        d1 = DIMS[p][0]
        s1[p, 1].wait_recv()
        f1[p, 1] = start(rel(d1, 3), d1, 1, A[p])
        s1[p, 3].wait_recv()
        f1[p, 3] = start(rel(d1, 1), d1, 3, B[p])
    for p in range(3):
        S2(p, 3); S2(p, 1)
        d1 = DIMS[p][0]
        cross(rel(d1, 3), F[p]); cross(rel(d1, 1), F[p])
    for p in range(3):
        f1[p, 1].wait_recv(); f1[p, 3].wait_recv()
        S2(p, 2)
        S3(p, 0)
        cross(rel(DIMS[p][0], 2), F[p])
    for o1 in OFFS:
        for p in range(3):
            d1, d2, d3 = DIMS[p]
            s2[p, o1, 1].wait_recv()
            f2[p, o1, 1] = start(moved(rel(d1, o1), d2, 3), d2, 1, A[p])
            s2[p, o1, 3].wait_recv()
            f2[p, o1, 3] = start(moved(rel(d1, o1), d2, 1), d2, 3, B[p])
    for p in range(3):
        d1, d2, d3 = DIMS[p]
        S3(p, 3); S3(p, 1)
        cross(allof(rel(d2, 3), d1), F[p]); cross(allof(rel(d2, 1), d1), F[p])
    for p in range(3):
        d1, d2, d3 = DIMS[p]
        for o1 in OFFS:
            f2[p, o1, 1].wait_recv(); f2[p, o1, 3].wait_recv()
        S3(p, 2)
        cross(allof(rel(d2, 2), d1), F[p])
    for o2 in OFFS:
        for p in range(3):
            d1, d2, d3 = DIMS[p]
            s3[p, o2, 1].wait_recv()
            sel = allof(moved(rel(d2, o2), d3, 3), d1)
            f3[p, o2, 1] = start(sel, d3, 1, A[p])
            cross(sel, F[p])
            s3[p, o2, 3].wait_recv()
            sel = allof(moved(rel(d2, o2), d3, 1), d1)
            f3[p, o2, 3] = start(sel, d3, 3, B[p])
            cross(sel, F[p])
    for o2 in OFFS:
        for p in range(3):
            d1, d2, d3 = DIMS[p]
            f3[p, o2, 1].wait_recv(); f3[p, o2, 3].wait_recv()
            cross(allof(moved(rel(d2, o2), d3, 2), d1), F[p])
    for c in cpend:
        c.wait_recv()
    for c in pend + cpend:
        c.wait_send()
    return nsem[0], ncs[0]

NS, NC = 108, 55


ORDER = (2, 1, 3, 0)
F32, BF16 = jnp.float32, jnp.bfloat16
FULL = [(c[0], c[2]) for c in CUT]; HA = [(c[0], c[1]) for c in CUT]; HB = [(c[1], c[2]) for c in CUT]

def barrier_all(pos, core, far):
    barrier = pltpu.get_barrier_semaphore()
    offs = (1, 2, 3) if far else (1, 3)
    for dim in range(3):
        for off in offs:
            pl.semaphore_signal(barrier, inc=1, device_id=dev(moved(pos, dim, off), core), device_id_type=MESH)
    pl.semaphore_signal(barrier, inc=1, device_id=dev(pos, 1 - core), device_id_type=MESH)
    pl.semaphore_wait(barrier, 3 * len(offs) + 1)

def pieces(p):
    lo, hi = FULL[p]
    out = []
    for b in range(5):
        r0, r1 = max(lo, b * 128), min(hi, b * 128 + 128)
        if r0 < r1:
            out.append((b, r0 - b * 128, r1 - b * 128))
    return out

def rows(r):
    return pl.ds(r[0], r[1] - r[0])

def reduce_scatter(proj, tab, H, W, Q, FR, SR, send, recv, pos, core):
    count = [0]
    pend = []
    tags = {}
    def ring_dim(p, lvl):
        return DIMS[p][2 - lvl]
    def hsel(p, lvl, grp, off):
        d1, d2, d3 = DIMS[p]
        sel = list(pos)
        if lvl == 0:
            sel[d1] = slice(None); sel[d2] = (pos[d2] + grp) % 4; sel[d3] = (pos[d3] + off) % 4
        elif lvl == 1:
            sel[d1] = (pos[d1] + grp) % 4; sel[d2] = (pos[d2] + off) % 4
        else:
            sel[d1] = (pos[d1] + off) % 4
        return tuple(sel)
    def rsel(p, lvl, grp):
        d1, d2, d3 = DIMS[p]
        if lvl == 0:
            return tuple(slice(None) if d == d1 else (pos[d2] + grp) % 4 for d in sorted((d1, d2)))
        if lvl == 1:
            return ((pos[d1] + grp) % 4,)
        return ()
    def wsel(p, lvl, grp, off):
        h = hsel(p, lvl, grp, off)
        return tuple(h[d] for d in sorted(DIMS[p][:2]))
    def source(p, lvl, grp, off, rr):
        if lvl == 0:
            return H.at[(*hsel(p, lvl, grp, off), rows(rr))]
        return (Q if lvl == 1 else W).at[(*wsel(p, lvl, grp, off), rows(rr))]
    def start(src, dst, p, lvl, off, tag):
        i = count[0]; count[0] += 1
        c = pltpu.make_async_remote_copy(src, dst, send.at[i], recv.at[i],
            device_id=dev(moved(pos, ring_dim(p, lvl), off), core), device_id_type=MESH)
        c.start(); pend.append(c); tags[tag] = c
    def send_f(p, lvl, grp):
        r = rsel(p, lvl, grp)
        start(source(p, lvl, grp, 2, HA[p]), FR[lvl].at[(*r, rows(HA[p]))], p, lvl, 1, ("f", p, lvl, grp, 1))
        start(source(p, lvl, grp, 2, HB[p]), FR[lvl].at[(*r, rows(HB[p]))], p, lvl, 3, ("f", p, lvl, grp, 3))
    def send_s(p, lvl, grp, off, half):
        r = rsel(p, lvl, grp)
        rr = (HA if half == 0 else HB)[p]
        start(source(p, lvl, grp, off, rr), SR[lvl].at[(0 if off == 1 else 1, *r, rows(rr))], p, lvl, off, ("s", p, lvl, grp, off, half))
    def chunks(h, r, body):
        if any(isinstance(s, slice) for s in h):
            def step(i, _):
                body(tuple(i if isinstance(s, slice) else s for s in h), tuple(i if isinstance(s, slice) else s for s in r))
                return 0
            lax.fori_loop(0, 4, step, 0)
        else:
            body(h, r)
    def fill(p, grp, off):
        def body(h, r):
            g0 = ((h[0] * 4 + h[1]) * 8 + h[2] * 2 + core) * 5
            for b, r0, r1 in pieces(p):
                rr = pl.ds(r0, r1 - r0)
                e = [tab[(g0 + b) * 4 + k] for k in range(4)]
                v = (proj[e[0], rr] + proj[e[1], rr]) + (proj[e[2], rr] + proj[e[3], rr])
                H[(*h, pl.ds(b * 128 + r0, r1 - r0))] = v
        h = hsel(p, 0, grp, off)
        chunks(h, h, body)
    def add_f(p, lvl, grp, off):
        rr = rows((HA if off == 1 else HB)[p])
        def body(h, r):
            if lvl == 0:
                H[(*h, rr)] = (H[(*h, rr)].astype(F32) + FR[0][(*r, rr)].astype(F32)).astype(BF16)
            elif lvl == 1:
                Q[(*h, rr)] = (W[(*h, rr)] + FR[1][(*r, rr)].astype(F32)).astype(BF16)
            else:
                W[(*h, rr)] = W[(*h, rr)] + FR[2][(*r, rr)]
        chunks((wsel if lvl else hsel)(p, lvl, grp, off), rsel(p, lvl, grp), body)
    def add_s(p, lvl, grp):
        rr = rows(FULL[p])
        def body(h, r):
            w = r if lvl == 0 else h
            own = H[(*h, rr)].astype(F32) if lvl == 0 else W[(*h, rr)]
            v = own + SR[lvl][(0, *r, rr)].astype(F32) + SR[lvl][(1, *r, rr)].astype(F32)
            W[(*w, rr)] = v
            if lvl == 0 and grp:
                Q[(*w, rr)] = v.astype(BF16)
        chunks((wsel if lvl else hsel)(p, lvl, grp, 0), rsel(p, lvl, grp), body)
    def middle(lvl, groups):
        for grp in groups:
            for p in range(3):
                tags["f", p, lvl, grp, 1].wait_recv()
                add_f(p, lvl, grp, 1)
                send_s(p, lvl, grp, 1, 0)
                tags["f", p, lvl, grp, 3].wait_recv()
                add_f(p, lvl, grp, 3)
                send_s(p, lvl, grp, 3, 1)
    def wait_s(p, lvl, grp):
        for off in (1, 3):
            for half in (0, 1):
                tags["s", p, lvl, grp, off, half].wait_recv()
    for grp in ORDER:
        for p in range(3):
            fill(p, grp, 2)
            send_f(p, 0, grp)
    for grp in ORDER:
        for p in range(3):
            fill(p, grp, 1)
            send_s(p, 0, grp, 1, 1)
            fill(p, grp, 3)
            send_s(p, 0, grp, 3, 0)
    middle(0, ORDER[:2])
    for grp in ORDER:
        for p in range(3):
            fill(p, grp, 0)
    middle(0, ORDER[2:])
    for grp in ORDER:
        for p in range(3):
            wait_s(p, 0, grp)
            add_s(p, 0, grp)
            for o1 in ORDER:
                if grp == 2:
                    send_f(p, 1, o1)
                elif grp == 1:
                    send_s(p, 1, o1, 1, 1)
                elif grp == 3:
                    send_s(p, 1, o1, 3, 0)
    middle(1, ORDER)
    for grp in ORDER:
        for p in range(3):
            wait_s(p, 1, grp)
            add_s(p, 1, grp)
            if grp == 2:
                send_f(p, 2, 0)
            elif grp == 1:
                send_s(p, 2, 0, 1, 1)
            elif grp == 3:
                send_s(p, 2, 0, 3, 0)
    middle(2, (0,))
    for p in range(3):
        wait_s(p, 2, 0)
    def finish():
        for c in pend:
            c.wait_send()
    assert count[0] == NR, count[0]
    def total(r0, r1):
        out = []
        for p in range(3):
            lo, hi = max(r0, FULL[p][0]), min(r1, FULL[p][1])
            if lo < hi:
                rr = pl.ds(lo, hi - lo)
                out.append(W[(*(pos[d] for d in sorted(DIMS[p][:2])), rr)] + SR[2][0, rr].astype(F32) + SR[2][1, rr].astype(F32))
        return jnp.concatenate(out, axis=0)
    return total, finish

NR = 162
def RS_SCRATCH(tb, tc):
    return [pltpu.VMEM((4, 4, 4, 640, 128), BF16), pltpu.VMEM((4, 4, 640, 128), F32), pltpu.VMEM((4, 4, 640, 128), BF16),
    pltpu.VMEM((4, 4, 640, 128), BF16), pltpu.VMEM((4, 640, 128), tb), pltpu.VMEM((640, 128), tc),
    pltpu.VMEM((2, 4, 4, 640, 128), BF16), pltpu.VMEM((2, 4, 640, 128), tb), pltpu.VMEM((2, 640, 128), tc),
    pltpu.SemaphoreType.DMA((NR,)), pltpu.SemaphoreType.DMA((NR,))]

def parts_of(half):
    a = -(-half // 24) * 8
    return ((0, a), (a, 2 * a), (2 * a, half))

def all_reduce(M, T, RB, send, recv, pos, core):
    R = M.shape[0]; half = R // 2
    pend = []
    other = dev(pos, 1 - core)
    n = [0]
    def copy(src, dst, to):
        i = n[0]; n[0] += 1
        c = pltpu.make_async_remote_copy(src, dst, send.at[i], recv.at[i], device_id=to, device_id_type=MESH)
        c.start(); pend.append(c); return c
    mine = pl.ds(pl.multiple_of(core * half, 8), half)
    theirs = pl.ds(pl.multiple_of((1 - core) * half, 8), half)
    first = copy(M.at[theirs], T.at[4], other)
    first.wait_recv()
    T[0] = M[mine] + T[4]
    P = parts_of(half)
    got = {}
    def sends(p, k):
        d = DIMS[p][k]
        me = pos[d]
        rr = rows(P[p])
        RB[k, me, rr] = T[k, rr]
        for off in (2, 1, 3):
            got[p, k, off] = copy(T.at[k, rr], RB.at[k, me, rr], dev(moved(pos, d, off), core))
    for p in range(3):
        sends(p, 0)
    for k in range(3):
        for p in range(3):
            rr = rows(P[p])
            for off in (1, 3, 2):
                got[p, k, off].wait_recv()
            T[k + 1, rr] = (RB[k, 0, rr] + RB[k, 1, rr]) + (RB[k, 2, rr] + RB[k, 3, rr])
            if k < 2:
                sends(p, k + 1)
    c = copy(T.at[3], T.at[5], other)
    M[mine] = T[3]
    c.wait_recv()
    first.wait_send()
    M[theirs] = T[5]
    for c in pend[1:]:
        c.wait_send()
    assert n[0] == NG

NG = 29
def AR_SCRATCH(R):
    return [pltpu.VMEM((6, R // 2, 128), F32), pltpu.VMEM((3, 4, R // 2, 128), F32),
            pltpu.SemaphoreType.DMA((NG,)), pltpu.SemaphoreType.DMA((NG,))]

def gram(a, b):
    return lax.dot_general(a, b, (((0,), (0,)), ((), ())), precision=lax.Precision.HIGHEST, preferred_element_type=F32)

def rs_kernel(m, proj, tab, d_ref, prior, image, grams, H, W, Q, FA, FB, FC, SA, SB, SC, send, recv, T, RB, gsend, grecv):
    pos, core = coords()
    barrier_all(pos, core, True)
    total, finish = reduce_scatter(proj, tab, H, W, Q, (FA, FB, FC), (SA, SB, SC), send, recv, pos, core)
    for b in range(5):
        rr = pl.ds(b * 128, 128)
        image[rr] = prior[rr] * d_ref[rr] + total(b * 128, b * 128 + 128).T
    grams[pl.ds(0, 128)] = gram(d_ref[...], image[...])
    if m > 1:
        grams[pl.ds(128, 128)] = gram(image[...], image[...])
        grams[pl.ds(256, 128)] = gram(d_ref[...], d_ref[...])
    all_reduce(grams, T, RB, gsend, grecv, pos, core)
    finish()

def rs_call(m, proj, tab, d, prior):
    V = pl.BlockSpec(memory_space=pltpu.VMEM)
    return pl.pallas_call(functools.partial(rs_kernel, m),
        out_shape=(jax.ShapeDtypeStruct((640, 128), F32), jax.ShapeDtypeStruct((128 * m, 128), F32)),
        in_specs=[V, pl.BlockSpec(memory_space=pltpu.SMEM), V, V], out_specs=(V, V),
        scratch_shapes=RS_SCRATCH(BF16, F32) + AR_SCRATCH(128 * m),
        compiler_params=pltpu.CompilerParams(collective_id=1 + m, has_side_effects=True, vmem_limit_bytes=34 << 20),
    )(proj, tab, d, prior)

F32, BF16 = jnp.float32, jnp.bfloat16
GROUP = 4
def nt(a, b):
    return lax.dot_general(a, b, (((1,), (1,)), ((), ())), preferred_element_type=F32).astype(BF16)
def nn(a, b):
    return lax.dot_general(a, b, (((1,), (0,)), ((), ())), preferred_element_type=F32).astype(BF16)

def k1_kernel(v_ref, idx_ref, panel_h, fac_h, proj, G, panel, fac, send, recv, csend, crecv, lsem, psend, precv):
    pos, core = coords()
    lp = pltpu.make_async_copy(panel_h, panel, lsem.at[0])
    lf = pltpu.make_async_copy(fac_h, fac, lsem.at[1])
    for b in range(5):
        G[pos[0], pos[1], pos[2], core, pl.ds(b * 128, 128)] = v_ref[pl.ds(b * 128, 128)].T.astype(BF16)
    entry_barrier(pos, core)
    lp.start(); lf.start()
    n = gather_all(G, send, recv, csend, crecv, pos, core)
    assert n == (NS, NC), n
    proj[256] = jnp.zeros((128, 128), BF16)
    lp.wait(); lf.wait()
    copies = lambda a: pltpu.make_async_remote_copy(proj.at[pl.ds(a * 8, 8)], proj.at[pl.ds(128 + a * 8, 8)],
        psend.at[a], precv.at[a], device_id=dev(pos, 1 - core), device_id_type=MESH)
    blocks = G.reshape(640, 128, 128)
    def arcs(i, _):
        mine = [i * GROUP + j for j in range(GROUP)]
        xs = [jnp.concatenate([blocks[idx_ref[a * 8 + k]] for k in range(8)], axis=1) for a in mine]
        xs = [nt(x, panel[a]) for x, a in zip(xs, mine)]
        xs = [nt(x, fac[a]) for x, a in zip(xs, mine)]
        xs = [nn(x, fac[a]) for x, a in zip(xs, mine)]
        for x, a in zip(xs, mine):
            y = nn(x, panel[a])
            for k in range(8):
                proj[a * 8 + k] = y[:, k * 128:(k + 1) * 128]
            copies(a).start()
        return 0
    lax.fori_loop(0, 16 // GROUP, arcs, 0)
    def fin(a, _):
        copies(a).wait()
        return 0
    lax.fori_loop(0, 16, fin, 0)

def k1_call(v, idx, panel, fac):
    V = pl.BlockSpec(memory_space=pltpu.VMEM); A = pl.BlockSpec(memory_space=pltpu.HBM)
    return pl.pallas_call(k1_kernel,
        out_shape=jax.ShapeDtypeStruct((257, 128, 128), BF16),
        in_specs=[V, pl.BlockSpec(memory_space=pltpu.SMEM), A, A], out_specs=V,
        scratch_shapes=[pltpu.VMEM((4, 4, 4, 2, 640, 128), BF16), pltpu.VMEM((16, 256, 1024), BF16), pltpu.VMEM((16, 256, 256), BF16),
            pltpu.SemaphoreType.DMA((NS,)), pltpu.SemaphoreType.DMA((NS,)),
            pltpu.SemaphoreType.DMA((NC,)), pltpu.SemaphoreType.DMA((NC,)), pltpu.SemaphoreType.DMA((2,)),
            pltpu.SemaphoreType.DMA((16,)), pltpu.SemaphoreType.DMA((16,))],
        compiler_params=pltpu.CompilerParams(collective_id=0, has_side_effects=True, vmem_limit_bytes=33 << 20),
    )(v, idx, pltpu.with_memory_space_constraint(panel, pltpu.HBM), pltpu.with_memory_space_constraint(fac, pltpu.HBM))

F32 = jnp.float32
def hdot(a, b, ca=1):
    return lax.dot_general(a, b, (((ca,), (0,)), ((), ())), precision=lax.Precision.HIGHEST, preferred_element_type=F32)

def negated_inverses(mats):
    lane = lax.broadcasted_iota(jnp.int32, (8, 128), 1)
    sub = lax.broadcasted_iota(jnp.int32, (8, 128), 0)
    wide = lax.broadcasted_iota(jnp.int32, (128, 128), 1)
    def sweep(_, carry):
        out = []
        tops = [a[:8] for a in carry]
        ws = list(tops)
        for j in range(0, 8, 2):
            for m in range(len(ws)):
                w = ws[m]
                col0 = jnp.broadcast_to(w[:, j:j + 1], (8, 128))
                col1 = jnp.broadcast_to(w[:, j + 1:j + 2], (8, 128))
                row0 = jnp.where(lane == j, 1.0, jnp.where(lane == j + 1, 0.0, jnp.broadcast_to(w[j:j + 1, :], (8, 128))))
                row1 = jnp.where(lane == j + 1, 1.0, jnp.where(lane == j, 0.0, jnp.broadcast_to(w[j + 1:j + 2, :], (8, 128))))
                a00 = jnp.broadcast_to(col0[j:j + 1, :], (8, 128))
                a10 = jnp.broadcast_to(col0[j + 1:j + 2, :], (8, 128))
                a01 = jnp.broadcast_to(col1[j:j + 1, :], (8, 128))
                a11 = jnp.broadcast_to(col1[j + 1:j + 2, :], (8, 128))
                inv = 1.0 / (a00 * a11 - a01 * a10)
                new0 = (a11 * row0 - a01 * row1) * inv
                new1 = (a00 * row1 - a10 * row0) * inv
                w = jnp.where((lane == j) | (lane == j + 1), 0.0, w) - col0 * new0 - col1 * new1
                ws[m] = jnp.where(sub == j, new0, jnp.where(sub == j + 1, new1, w))
        for a, p, w in zip(carry, tops, ws):
            m = hdot(jnp.where(lane < 8, 0.0, p), w, 0)
            rest = jnp.where(wide < 8, m, a - m)
            first = jnp.where(lane < 8, -w, w)
            out.append(pltpu.roll(jnp.concatenate([rest[8:], first], axis=0), 120, 1))
        return tuple(out)
    return lax.fori_loop(0, 16, sweep, tuple(mats))

def sym(a):
    return (a + a.T) * 0.5

def first_kernel(grams, b, image, x, r, d, new):
    c, g2, g0 = grams[pl.ds(0, 128)], grams[pl.ds(128, 128)], grams[pl.ds(256, 128)]
    ci, gi = negated_inverses((sym(c), sym(g0)))
    alpha = -hdot(ci, g0)
    ca = hdot(c, alpha)
    ng = g0 - ca - ca.T + hdot(alpha, hdot(g2, alpha), 0)
    beta = -hdot(gi, ng)
    new[...] = ng
    bb = b[...]
    x[...] = hdot(bb, alpha)
    rr = bb - hdot(image[...], alpha)
    r[...] = rr
    d[...] = rr + hdot(bb, beta)

def last_kernel(c, new, x0, r0, d, image, x, r):
    (ci,) = negated_inverses((sym(c[...]),))
    alpha = -hdot(ci, new[...])
    x[...] = x0[...] + hdot(d[...], alpha)
    r[...] = r0[...] - hdot(image[...], alpha)

def first_call(grams, b, image):
    big, small = jax.ShapeDtypeStruct((640, 128), F32), jax.ShapeDtypeStruct((128, 128), F32)
    V = pl.BlockSpec(memory_space=pltpu.VMEM)
    return pl.pallas_call(first_kernel, out_shape=(big, big, big, small), in_specs=[V] * 3, out_specs=(V,) * 4,
        compiler_params=pltpu.CompilerParams(vmem_limit_bytes=16 << 20))(grams, b, image)

def last_call(c, new, x0, r0, d, image):
    big = jax.ShapeDtypeStruct((640, 128), F32)
    V = pl.BlockSpec(memory_space=pltpu.VMEM)
    return pl.pallas_call(last_kernel, out_shape=(big, big), in_specs=[V] * 6, out_specs=(V,) * 2,
        compiler_params=pltpu.CompilerParams(vmem_limit_bytes=16 << 20))(c, new, x0, r0, d, image)

def tables(owner, block, me, core):
    g = owner * 5 + block
    mine = lax.dynamic_slice_in_dim(g.reshape(128, 128), me, 1, 0).reshape(128)
    theirs = lax.dynamic_slice_in_dim(g.reshape(128, 128), me + 1 - 2 * core, 1, 0).reshape(128)
    def two(row, base):
        e = jnp.arange(128, dtype=jnp.int32)
        hit = row[None, :] == jnp.arange(640, dtype=jnp.int32)[:, None]
        first = jnp.min(jnp.where(hit, e[None], 999), axis=1)
        last = jnp.max(jnp.where(hit, e[None], -1), axis=1)
        return jnp.where(first < 999, first + base, 256), jnp.where(last > first, last + base, 256)
    t = jnp.stack([*two(mine, 0), *two(theirs, 128)], axis=1).reshape(-1).astype(jnp.int32)
    return mine, t
def per_device(right_side, prior_diag, inv_factor, coupling_panel, owner, block):
    me = lax.axis_index(("arc", "vec"))
    core = me % 2
    idx, tab = tables(owner, block, me, core)
    b = right_side.reshape(640, 128)
    prior = jnp.broadcast_to(prior_diag.reshape(640, 1), (640, 128))
    proj = k1_call(b, idx, coupling_panel, inv_factor)
    image, grams = rs_call(3, proj, tab, b, prior)
    x, r, d, new = first_call(grams, b, image)
    proj = k1_call(d, idx, coupling_panel, inv_factor)
    image, c = rs_call(1, proj, tab, d, prior)
    x, r = last_call(c, new, x, r, d, image)
    return x.reshape(5, 128, 128), r.reshape(5, 128, 128)
def solution(mesh):
    ins = (P(("arc", "vec"), None, None), P(("arc", "vec"), None), P(("arc", "vec"), None, None), P(("arc", "vec"), None, None), P(), P())
    outs = (P(("arc", "vec"), None, None), P(("arc", "vec"), None, None))
    return jax.shard_map(per_device, mesh=mesh, in_specs=ins, out_specs=outs, check_vma=False)
```

```python
import functools
import jax
import jax.numpy as jnp
from jax import lax
from jax.experimental import pallas as pl
from jax.experimental.pallas import tpu as pltpu
from jax.sharding import PartitionSpec as P
MESH = pl.DeviceIdType.MESH
DIMS = ((0, 1, 2), (1, 2, 0), (2, 0, 1))
CUT = ((0, 112, 208), (208, 320, 432), (432, 528, 640))
OFFS = (0, 3, 1, 2)

def coords():
    arc, vec = lax.axis_index("arc"), lax.axis_index("vec")
    return (arc // 4, arc % 4, vec // 2), vec % 2

def dev(pos, core):
    return (pos[0] * 4 + pos[1], pos[2] * 2 + core)

def moved(pos, dim, off):
    return tuple((p + off) % 4 if d == dim else p for d, p in enumerate(pos))

def entry_barrier(pos, core):
    barrier = pltpu.get_barrier_semaphore()
    for dim in range(3):
        for off in (1, 3):
            pl.semaphore_signal(barrier, inc=1, device_id=dev(moved(pos, dim, off), core), device_id_type=MESH)
    pl.semaphore_signal(barrier, inc=1, device_id=dev(pos, 1 - core), device_id_type=MESH)
    return lambda: pl.semaphore_wait(barrier, 7)

def gather_all(G, send, recv, csend, crecv, pos, core):
    pend = []
    cpend = []
    nsem = [0]
    ncs = [0]
    def at(sel, cc, rows):
        return G.at[sel[0], sel[1], sel[2], cc, pl.ds(rows[0], rows[1] - rows[0])]
    def make(sel_src, dim, off, rows):
        i = nsem[0]; nsem[0] += 1
        ref = at(sel_src, core, rows)
        return pltpu.make_async_remote_copy(ref, ref, send.at[i], recv.at[i],
            device_id=dev(moved(pos, dim, off), core), device_id_type=MESH)
    def start(sel, dim, off, rows):
        c = make(sel, dim, off, rows); c.start(); pend.append(c); return c
    def cross(sel, rows):
        i = ncs[0]; ncs[0] += 1
        ref = at(sel, core, rows)
        c = pltpu.make_async_remote_copy(ref, ref, csend.at[i], crecv.at[i],
            device_id=dev(pos, 1 - core), device_id_type=MESH)
        c.start(); cpend.append(c)
    def rel(dim, off):
        return moved(pos, dim, off)
    def allof(sel, *dims):
        return tuple(slice(None) if d in dims else s for d, s in enumerate(sel))
    A = [(c[0], c[1]) for c in CUT]; B = [(c[1], c[2]) for c in CUT]; F = [(c[0], c[2]) for c in CUT]
    s1 = {}; f1 = {}; s2 = {}; f2 = {}; s3 = {}; f3 = {}
    def S2(p, o1):
        d1, d2, d3 = DIMS[p]
        for off in (1, 3):
            s2[p, o1, off] = start(moved(pos, d1, o1), d2, off, F[p])
    def S3(p, o2):
        d1, d2, d3 = DIMS[p]
        for off in (1, 3):
            s3[p, o2, off] = start(allof(moved(pos, d2, o2), d1), d3, off, F[p])
    for p in range(3):
        d1 = DIMS[p][0]
        for off in (1, 3):
            s1[p, off] = start(pos, d1, off, F[p])
    def S3one(p, o1):
        d1, d2, d3 = DIMS[p]
        for off in (1, 3):
            s3[p, 0, off, o1] = start(moved(pos, d1, o1), d3, off, F[p])
    for p in range(3):
        S2(p, 0)
    for p in range(3):
        S3one(p, 0)
    cross(pos, (0, 640))
    for p in range(3):
        d1 = DIMS[p][0]
        s1[p, 1].wait_recv()
        f1[p, 1] = start(rel(d1, 3), d1, 1, A[p])
        s1[p, 3].wait_recv()
        f1[p, 3] = start(rel(d1, 1), d1, 3, B[p])
    for p in range(3):
        S2(p, 3); S2(p, 1)
        d1 = DIMS[p][0]
        S3one(p, 3); S3one(p, 1)
        cross(rel(d1, 3), F[p]); cross(rel(d1, 1), F[p])
    for p in range(3):
        f1[p, 1].wait_recv(); f1[p, 3].wait_recv()
        S2(p, 2)
        S3one(p, 2)
        cross(rel(DIMS[p][0], 2), F[p])
    for o1 in OFFS:
        for p in range(3):
            d1, d2, d3 = DIMS[p]
            s2[p, o1, 1].wait_recv()
            f2[p, o1, 1] = start(moved(rel(d1, o1), d2, 3), d2, 1, A[p])
            s2[p, o1, 3].wait_recv()
            f2[p, o1, 3] = start(moved(rel(d1, o1), d2, 1), d2, 3, B[p])
    for p in range(3):
        d1, d2, d3 = DIMS[p]
        S3(p, 3); S3(p, 1)
        cross(allof(rel(d2, 3), d1), F[p]); cross(allof(rel(d2, 1), d1), F[p])
    for p in range(3):
        d1, d2, d3 = DIMS[p]
        for o1 in OFFS:
            f2[p, o1, 1].wait_recv(); f2[p, o1, 3].wait_recv()
        S3(p, 2)
        cross(allof(rel(d2, 2), d1), F[p])
    def arrived(p, o2, off):
        for c in ([s3[p, 0, off, o1] for o1 in OFFS] if o2 == 0 else [s3[p, o2, off]]):
            c.wait_recv()
    for o2 in OFFS:
        for p in range(3):
            d1, d2, d3 = DIMS[p]
            arrived(p, o2, 1)
            sel = allof(moved(rel(d2, o2), d3, 3), d1)
            f3[p, o2, 1] = start(sel, d3, 1, A[p])
            cross(sel, F[p])
            arrived(p, o2, 3)
            sel = allof(moved(rel(d2, o2), d3, 1), d1)
            f3[p, o2, 3] = start(sel, d3, 3, B[p])
            cross(sel, F[p])
    for o2 in OFFS:
        for p in range(3):
            d1, d2, d3 = DIMS[p]
            f3[p, o2, 1].wait_recv(); f3[p, o2, 3].wait_recv()
            cross(allof(moved(rel(d2, o2), d3, 2), d1), F[p])
    for c in cpend:
        c.wait_recv()
    for c in pend + cpend:
        c.wait_send()
    return nsem[0], ncs[0]

NS, NC = 126, 55


ORDER = (2, 1, 3, 0)
F32, BF16 = jnp.float32, jnp.bfloat16
FULL = [(c[0], c[2]) for c in CUT]; HA = [(c[0], c[1]) for c in CUT]; HB = [(c[1], c[2]) for c in CUT]

def barrier_all(pos, core):
    barrier = pltpu.get_barrier_semaphore()
    for dim in range(3):
        for off in (1, 2, 3):
            for cc in (0, 1):
                pl.semaphore_signal(barrier, inc=1, device_id=dev(moved(pos, dim, off), cc), device_id_type=MESH)
    pl.semaphore_signal(barrier, inc=1, device_id=dev(pos, 1 - core), device_id_type=MESH)
    return lambda: pl.semaphore_wait(barrier, 19)

def pieces(p):
    lo, hi = FULL[p]
    out = []
    for b in range(5):
        r0, r1 = max(lo, b * 128), min(hi, b * 128 + 128)
        if r0 < r1:
            out.append((b, r0 - b * 128, r1 - b * 128))
    return out

def rows(r):
    return pl.ds(r[0], r[1] - r[0])

def reduce_scatter(proj, tab, H, W, Q, FR, SR, send, recv, pos, core, entered):
    count = [0]
    pend = []
    tags = {}
    def ring_dim(p, lvl):
        return DIMS[p][2 - lvl]
    def hsel(p, lvl, grp, off):
        d1, d2, d3 = DIMS[p]
        sel = list(pos)
        if lvl == 0:
            sel[d1] = slice(None); sel[d2] = (pos[d2] + grp) % 4; sel[d3] = (pos[d3] + off) % 4
        elif lvl == 1:
            sel[d1] = (pos[d1] + grp) % 4; sel[d2] = (pos[d2] + off) % 4
        else:
            sel[d1] = (pos[d1] + off) % 4
        return tuple(sel)
    def rsel(p, lvl, grp):
        d1, d2, d3 = DIMS[p]
        if lvl == 0:
            return tuple(slice(None) if d == d1 else (pos[d2] + grp) % 4 for d in sorted((d1, d2)))
        if lvl == 1:
            return ((pos[d1] + grp) % 4,)
        return ()
    def wsel(p, lvl, grp, off):
        h = hsel(p, lvl, grp, off)
        return tuple(h[d] for d in sorted(DIMS[p][:2]))
    def source(p, lvl, grp, off, rr):
        if lvl == 0:
            return H.at[(*hsel(p, lvl, grp, off), rows(rr))]
        return (Q if lvl == 1 else W).at[(*wsel(p, lvl, grp, off), rows(rr))]
    def start(src, dst, p, lvl, off, tag):
        i = count[0]; count[0] += 1
        c = pltpu.make_async_remote_copy(src, dst, send.at[i], recv.at[i],
            device_id=dev(moved(pos, ring_dim(p, lvl), off), core), device_id_type=MESH)
        c.start(); pend.append(c); tags[tag] = c
    def send_f(p, lvl, grp):
        r = rsel(p, lvl, grp)
        start(source(p, lvl, grp, 2, HA[p]), FR[lvl].at[(*r, rows(HA[p]))], p, lvl, 1, ("f", p, lvl, grp, 1))
        start(source(p, lvl, grp, 2, HB[p]), FR[lvl].at[(*r, rows(HB[p]))], p, lvl, 3, ("f", p, lvl, grp, 3))
    def send_s(p, lvl, grp, off, half):
        r = rsel(p, lvl, grp)
        rr = (HA if half == 0 else HB)[p]
        start(source(p, lvl, grp, off, rr), SR[lvl].at[(0 if off == 1 else 1, *r, rows(rr))], p, lvl, off, ("s", p, lvl, grp, off, half))
    def chunks(h, r, body):
        if any(isinstance(s, slice) for s in h):
            def step(i, _):
                body(tuple(i if isinstance(s, slice) else s for s in h), tuple(i if isinstance(s, slice) else s for s in r))
                return 0
            lax.fori_loop(0, 4, step, 0)
        else:
            body(h, r)
    def fill(p, grp, off):
        def body(h, r):
            g0 = ((h[0] * 4 + h[1]) * 8 + h[2] * 2 + core) * 5
            for b, r0, r1 in pieces(p):
                rr = pl.ds(r0, r1 - r0)
                e = [tab[(g0 + b) * 4 + k] for k in range(4)]
                v = (proj[e[0], rr] + proj[e[1], rr]) + (proj[e[2], rr] + proj[e[3], rr])
                H[(*h, pl.ds(b * 128 + r0, r1 - r0))] = v
        h = hsel(p, 0, grp, off)
        chunks(h, h, body)
    def add_f(p, lvl, grp, off):
        rr = rows((HA if off == 1 else HB)[p])
        def body(h, r):
            if lvl == 0:
                H[(*h, rr)] = (H[(*h, rr)].astype(F32) + FR[0][(*r, rr)].astype(F32)).astype(BF16)
            elif lvl == 1:
                Q[(*h, rr)] = (W[(*h, rr)] + FR[1][(*r, rr)].astype(F32)).astype(BF16)
            else:
                W[(*h, rr)] = W[(*h, rr)] + FR[2][(*r, rr)]
        chunks((wsel if lvl else hsel)(p, lvl, grp, off), rsel(p, lvl, grp), body)
    def add_s(p, lvl, grp):
        rr = rows(FULL[p])
        def body(h, r):
            w = r if lvl == 0 else h
            own = H[(*h, rr)].astype(F32) if lvl == 0 else W[(*h, rr)]
            v = own + SR[lvl][(0, *r, rr)].astype(F32) + SR[lvl][(1, *r, rr)].astype(F32)
            W[(*w, rr)] = v
            if lvl == 0 and grp:
                Q[(*w, rr)] = v.astype(BF16)
        chunks((wsel if lvl else hsel)(p, lvl, grp, 0), rsel(p, lvl, grp), body)
    def middle(lvl, groups):
        for grp in groups:
            for p in range(3):
                tags["f", p, lvl, grp, 1].wait_recv()
                add_f(p, lvl, grp, 1)
                send_s(p, lvl, grp, 1, 0)
                tags["f", p, lvl, grp, 3].wait_recv()
                add_f(p, lvl, grp, 3)
                send_s(p, lvl, grp, 3, 1)
    def wait_s(p, lvl, grp):
        for off in (1, 3):
            for half in (0, 1):
                tags["s", p, lvl, grp, off, half].wait_recv()
    for grp in ORDER:
        for p in range(3):
            fill(p, grp, 2)
            if grp == ORDER[0] and p == 0:
                entered()
            send_f(p, 0, grp)
    for grp in ORDER:
        for p in range(3):
            fill(p, grp, 1)
            send_s(p, 0, grp, 1, 1)
            fill(p, grp, 3)
            send_s(p, 0, grp, 3, 0)
    middle(0, ORDER[:2])
    for grp in ORDER:
        for p in range(3):
            fill(p, grp, 0)
    middle(0, ORDER[2:])
    for grp in ORDER:
        for p in range(3):
            wait_s(p, 0, grp)
            add_s(p, 0, grp)
            for o1 in ORDER:
                if grp == 2:
                    send_f(p, 1, o1)
                elif grp == 1:
                    send_s(p, 1, o1, 1, 1)
                elif grp == 3:
                    send_s(p, 1, o1, 3, 0)
    middle(1, ORDER)
    for grp in ORDER:
        for p in range(3):
            wait_s(p, 1, grp)
            add_s(p, 1, grp)
            if grp == 2:
                send_f(p, 2, 0)
            elif grp == 1:
                send_s(p, 2, 0, 1, 1)
            elif grp == 3:
                send_s(p, 2, 0, 3, 0)
    middle(2, (0,))
    for p in range(3):
        wait_s(p, 2, 0)
    def finish():
        for c in pend:
            c.wait_send()
    assert count[0] == NR, count[0]
    def total(r0, r1):
        out = []
        for p in range(3):
            lo, hi = max(r0, FULL[p][0]), min(r1, FULL[p][1])
            if lo < hi:
                rr = pl.ds(lo, hi - lo)
                out.append(W[(*(pos[d] for d in sorted(DIMS[p][:2])), rr)] + SR[2][0, rr].astype(F32) + SR[2][1, rr].astype(F32))
        return jnp.concatenate(out, axis=0)
    return total, finish

NR = 162
def RS_SCRATCH(tb, tc):
    return [pltpu.VMEM((4, 4, 4, 640, 128), BF16), pltpu.VMEM((4, 4, 640, 128), F32), pltpu.VMEM((4, 4, 640, 128), BF16),
    pltpu.VMEM((4, 4, 640, 128), BF16), pltpu.VMEM((4, 640, 128), tb), pltpu.VMEM((640, 128), tc),
    pltpu.VMEM((2, 4, 4, 640, 128), BF16), pltpu.VMEM((2, 4, 640, 128), tb), pltpu.VMEM((2, 640, 128), tc),
    pltpu.SemaphoreType.DMA((NR,)), pltpu.SemaphoreType.DMA((NR,))]

def parts_of(half):
    a = -(-half // 24) * 8
    return ((0, a), (a, 2 * a), (2 * a, half))

def all_reduce(M, OUT, T, R0, R1, R2, send, recv, pos, core):
    half = M.shape[0] // 2
    parts = parts_of(half)
    pend = []
    def copy(src, dst, to):
        i = len(pend)
        c = pltpu.make_async_remote_copy(src, dst, send.at[i], recv.at[i], device_id=to, device_id_type=MESH)
        c.start(); pend.append(c); return c
    def part(cc, r):
        return pl.ds(pl.multiple_of(cc * half + r[0], 8), r[1] - r[0])
    def steps(p, k):
        d = DIMS[p][k]
        return pos[d], [(o, j) for o in ((2, 1, 3, 0) if k != 1 else (2, 1, 3)) for j in ((0, 1) if k != 1 else (0,)) if o or j], d
    got = {}
    def send_step(p, k):
        me, moves, d = steps(p, k)
        rr = rows(parts[p])
        slot = me * 2 + core if k == 0 else me if k == 1 else core * 4 + me
        buf = (R0, R1, R2)[k]
        buf[slot, rr] = M[part(core, parts[p])] if k == 0 else T[k - 1, rr]
        for o, j in moves:
            to = 1 - core if j else core
            src = M.at[part(to, parts[p])] if k == 0 else T.at[k - 1, rr]
            got[p, k, o, j] = copy(src, buf.at[slot, rr], dev(moved(pos, d, o), to))
    def take(p, k):
        for o, j in reversed(steps(p, k)[1]):
            got[p, k, o, j].wait_recv()
    def quad(buf, i, rr):
        return (buf[i, rr] + buf[i + 1, rr]) + (buf[i + 2, rr] + buf[i + 3, rr])
    for p in range(3):
        send_step(p, 0)
    for k in range(3):
        for p in range(3):
            rr = rows(parts[p])
            take(p, k)
            if k == 0:
                T[0, rr] = quad(R0, 0, rr) + quad(R0, 4, rr)
            elif k == 1:
                T[1, rr] = quad(R1, 0, rr)
            else:
                for h in range(2):
                    OUT[pl.ds(h * half + parts[p][0], parts[p][1] - parts[p][0])] = quad(R2, 4 * h, rr)
            if k < 2:
                send_step(p, k + 1)
    for c in pend:
        c.wait_send()
    assert len(pend) == NG, len(pend)

NG = 51
def AR_SCRATCH(R):
    return [pltpu.VMEM((R, 128), F32), pltpu.VMEM((2, R // 2, 128), F32), pltpu.VMEM((8, R // 2, 128), F32),
            pltpu.VMEM((4, R // 2, 128), F32), pltpu.VMEM((8, R // 2, 128), F32),
            pltpu.SemaphoreType.DMA((NG,)), pltpu.SemaphoreType.DMA((NG,))]

def gram(a, b):
    return lax.dot_general(a, b, (((0,), (0,)), ((), ())), precision=lax.Precision.HIGHEST, preferred_element_type=F32)

def rs_kernel(m, proj, tab, d_ref, prior, image, grams, H, W, Q, FA, FB, FC, SA, SB, SC, send, recv, M, T, R0, R1, R2, gsend, grecv):
    pos, core = coords()
    entered = barrier_all(pos, core)
    total, finish = reduce_scatter(proj, tab, H, W, Q, (FA, FB, FC), (SA, SB, SC), send, recv, pos, core, entered)
    for b in range(5):
        rr = pl.ds(b * 128, 128)
        image[rr] = prior[rr] * d_ref[rr] + total(b * 128, b * 128 + 128).T
    M[pl.ds(0, 128)] = gram(d_ref[...], image[...])
    if m > 1:
        M[pl.ds(128, 128)] = gram(image[...], image[...])
        M[pl.ds(256, 128)] = gram(d_ref[...], d_ref[...])
    all_reduce(M, grams, T, R0, R1, R2, gsend, grecv, pos, core)
    finish()

def rs_call(m, proj, tab, d, prior):
    V = pl.BlockSpec(memory_space=pltpu.VMEM)
    return pl.pallas_call(functools.partial(rs_kernel, m),
        out_shape=(jax.ShapeDtypeStruct((640, 128), F32), jax.ShapeDtypeStruct((128 * m, 128), F32)),
        in_specs=[V, pl.BlockSpec(memory_space=pltpu.SMEM), V, V], out_specs=(V, V),
        scratch_shapes=RS_SCRATCH(BF16, F32) + AR_SCRATCH(128 * m),
        compiler_params=pltpu.CompilerParams(collective_id=1 + m, has_side_effects=True, vmem_limit_bytes=36 << 20),
    )(proj, tab, d, prior)

F32, BF16 = jnp.float32, jnp.bfloat16
GROUP = 4
def nt(a, b):
    return lax.dot_general(a, b, (((1,), (1,)), ((), ())), preferred_element_type=F32).astype(BF16)
def nn(a, b):
    return lax.dot_general(a, b, (((1,), (0,)), ((), ())), preferred_element_type=F32).astype(BF16)

def k1_kernel(v_ref, idx_ref, panel_h, fac_h, proj, G, panel, fac, send, recv, csend, crecv, lsem, psend, precv):
    pos, core = coords()
    lp = pltpu.make_async_copy(panel_h, panel, lsem.at[0])
    lf = pltpu.make_async_copy(fac_h, fac, lsem.at[1])
    entered = entry_barrier(pos, core)
    lp.start(); lf.start()
    for b in range(5):
        G[pos[0], pos[1], pos[2], core, pl.ds(b * 128, 128)] = v_ref[pl.ds(b * 128, 128)].T.astype(BF16)
    entered()
    n = gather_all(G, send, recv, csend, crecv, pos, core)
    assert n == (NS, NC), n
    proj[256] = jnp.zeros((128, 128), BF16)
    lp.wait(); lf.wait()
    copies = lambda a: pltpu.make_async_remote_copy(proj.at[pl.ds(a * 8, 8)], proj.at[pl.ds(128 + a * 8, 8)],
        psend.at[a], precv.at[a], device_id=dev(pos, 1 - core), device_id_type=MESH)
    blocks = G.reshape(640, 128, 128)
    def arcs(i, _):
        mine = [i * GROUP + j for j in range(GROUP)]
        xs = [jnp.concatenate([blocks[idx_ref[a * 8 + k]] for k in range(8)], axis=1) for a in mine]
        xs = [nt(x, panel[a]) for x, a in zip(xs, mine)]
        xs = [nt(x, fac[a]) for x, a in zip(xs, mine)]
        xs = [nn(x, fac[a]) for x, a in zip(xs, mine)]
        for x, a in zip(xs, mine):
            y = nn(x, panel[a])
            for k in range(8):
                proj[a * 8 + k] = y[:, k * 128:(k + 1) * 128]
            copies(a).start()
        return 0
    lax.fori_loop(0, 16 // GROUP, arcs, 0)
    def fin(a, _):
        copies(a).wait()
        return 0
    lax.fori_loop(0, 16, fin, 0)

def k1_call(v, idx, panel, fac):
    V = pl.BlockSpec(memory_space=pltpu.VMEM); A = pl.BlockSpec(memory_space=pltpu.HBM)
    return pl.pallas_call(k1_kernel,
        out_shape=jax.ShapeDtypeStruct((257, 128, 128), BF16),
        in_specs=[V, pl.BlockSpec(memory_space=pltpu.SMEM), A, A], out_specs=V,
        scratch_shapes=[pltpu.VMEM((4, 4, 4, 2, 640, 128), BF16), pltpu.VMEM((16, 256, 1024), BF16), pltpu.VMEM((16, 256, 256), BF16),
            pltpu.SemaphoreType.DMA((NS,)), pltpu.SemaphoreType.DMA((NS,)),
            pltpu.SemaphoreType.DMA((NC,)), pltpu.SemaphoreType.DMA((NC,)), pltpu.SemaphoreType.DMA((2,)),
            pltpu.SemaphoreType.DMA((16,)), pltpu.SemaphoreType.DMA((16,))],
        compiler_params=pltpu.CompilerParams(collective_id=0, has_side_effects=True, vmem_limit_bytes=33 << 20),
    )(v, idx, pltpu.with_memory_space_constraint(panel, pltpu.HBM), pltpu.with_memory_space_constraint(fac, pltpu.HBM))

F32 = jnp.float32
def hdot(a, b, ca=1):
    return lax.dot_general(a, b, (((ca,), (0,)), ((), ())), precision=lax.Precision.HIGHEST, preferred_element_type=F32)

def negated_inverses(mats):
    lane = lax.broadcasted_iota(jnp.int32, (8, 128), 1)
    sub = lax.broadcasted_iota(jnp.int32, (8, 128), 0)
    wide = lax.broadcasted_iota(jnp.int32, (128, 128), 1)
    def sweep(_, carry):
        out = []
        tops = [a[:8] for a in carry]
        ws = list(tops)
        for j in range(0, 8, 2):
            for m in range(len(ws)):
                w = ws[m]
                col0 = jnp.broadcast_to(w[:, j:j + 1], (8, 128))
                col1 = jnp.broadcast_to(w[:, j + 1:j + 2], (8, 128))
                row0 = jnp.where(lane == j, 1.0, jnp.where(lane == j + 1, 0.0, jnp.broadcast_to(w[j:j + 1, :], (8, 128))))
                row1 = jnp.where(lane == j + 1, 1.0, jnp.where(lane == j, 0.0, jnp.broadcast_to(w[j + 1:j + 2, :], (8, 128))))
                a00 = jnp.broadcast_to(col0[j:j + 1, :], (8, 128))
                a10 = jnp.broadcast_to(col0[j + 1:j + 2, :], (8, 128))
                a01 = jnp.broadcast_to(col1[j:j + 1, :], (8, 128))
                a11 = jnp.broadcast_to(col1[j + 1:j + 2, :], (8, 128))
                inv = 1.0 / (a00 * a11 - a01 * a10)
                new0 = (a11 * row0 - a01 * row1) * inv
                new1 = (a00 * row1 - a10 * row0) * inv
                w = jnp.where((lane == j) | (lane == j + 1), 0.0, w) - col0 * new0 - col1 * new1
                ws[m] = jnp.where(sub == j, new0, jnp.where(sub == j + 1, new1, w))
        for a, p, w in zip(carry, tops, ws):
            m = hdot(jnp.where(lane < 8, 0.0, p), w, 0)
            rest = jnp.where(wide < 8, m, a - m)
            first = jnp.where(lane < 8, -w, w)
            out.append(pltpu.roll(jnp.concatenate([rest[8:], first], axis=0), 120, 1))
        return tuple(out)
    return lax.fori_loop(0, 16, sweep, tuple(mats))

def sym(a):
    return (a + a.T) * 0.5

def first_kernel(grams, b, image, x, r, d, new):
    c, g2, g0 = grams[pl.ds(0, 128)], grams[pl.ds(128, 128)], grams[pl.ds(256, 128)]
    ci, gi = negated_inverses((sym(c), sym(g0)))
    alpha = -hdot(ci, g0)
    ca = hdot(c, alpha)
    ng = g0 - ca - ca.T + hdot(alpha, hdot(g2, alpha), 0)
    beta = -hdot(gi, ng)
    new[...] = ng
    bb = b[...]
    x[...] = hdot(bb, alpha)
    rr = bb - hdot(image[...], alpha)
    r[...] = rr
    d[...] = rr + hdot(bb, beta)

def last_kernel(c, new, x0, r0, d, image, x, r):
    (ci,) = negated_inverses((sym(c[...]),))
    alpha = -hdot(ci, new[...])
    x[...] = x0[...] + hdot(d[...], alpha)
    r[...] = r0[...] - hdot(image[...], alpha)

def first_call(grams, b, image):
    big, small = jax.ShapeDtypeStruct((640, 128), F32), jax.ShapeDtypeStruct((128, 128), F32)
    V = pl.BlockSpec(memory_space=pltpu.VMEM)
    return pl.pallas_call(first_kernel, out_shape=(big, big, big, small), in_specs=[V] * 3, out_specs=(V,) * 4,
        compiler_params=pltpu.CompilerParams(vmem_limit_bytes=16 << 20))(grams, b, image)

def last_call(c, new, x0, r0, d, image):
    big = jax.ShapeDtypeStruct((640, 128), F32)
    V = pl.BlockSpec(memory_space=pltpu.VMEM)
    return pl.pallas_call(last_kernel, out_shape=(big, big), in_specs=[V] * 6, out_specs=(V,) * 2,
        compiler_params=pltpu.CompilerParams(vmem_limit_bytes=16 << 20))(c, new, x0, r0, d, image)

def tables(owner, block, me, core):
    g = owner * 5 + block
    mine = lax.dynamic_slice_in_dim(g.reshape(128, 128), me, 1, 0).reshape(128)
    theirs = lax.dynamic_slice_in_dim(g.reshape(128, 128), me + 1 - 2 * core, 1, 0).reshape(128)
    def two(row, base):
        e = jnp.arange(128, dtype=jnp.int32)
        hit = row[None, :] == jnp.arange(640, dtype=jnp.int32)[:, None]
        first = jnp.min(jnp.where(hit, e[None], 999), axis=1)
        last = jnp.max(jnp.where(hit, e[None], -1), axis=1)
        return jnp.where(first < 999, first + base, 256), jnp.where(last > first, last + base, 256)
    t = jnp.stack([*two(mine, 0), *two(theirs, 128)], axis=1).reshape(-1).astype(jnp.int32)
    return mine, t
def per_device(right_side, prior_diag, inv_factor, coupling_panel, owner, block):
    me = lax.axis_index(("arc", "vec"))
    core = me % 2
    idx, tab = tables(owner, block, me, core)
    b = right_side.reshape(640, 128)
    prior = jnp.broadcast_to(prior_diag.reshape(640, 1), (640, 128))
    proj = k1_call(b, idx, coupling_panel, inv_factor)
    image, grams = rs_call(3, proj, tab, b, prior)
    x, r, d, new = first_call(grams, b, image)
    proj = k1_call(d, idx, coupling_panel, inv_factor)
    image, c = rs_call(1, proj, tab, d, prior)
    x, r = last_call(c, new, x, r, d, image)
    return x.reshape(5, 128, 128), r.reshape(5, 128, 128)
def solution(mesh):
    ins = (P(("arc", "vec"), None, None), P(("arc", "vec"), None), P(("arc", "vec"), None, None), P(("arc", "vec"), None, None), P(), P())
    outs = (P(("arc", "vec"), None, None), P(("arc", "vec"), None, None))
    return jax.shard_map(per_device, mesh=mesh, in_specs=ins, out_specs=outs, check_vma=False)
```

```python
import functools
import jax
import jax.numpy as jnp
from jax import lax
from jax.experimental import pallas as pl
from jax.experimental.pallas import tpu as pltpu
from jax.sharding import PartitionSpec as P
MESH = pl.DeviceIdType.MESH
DIMS = ((0, 1, 2), (1, 2, 0), (2, 0, 1))
CUT = ((0, 112, 208), (208, 320, 432), (432, 528, 640))
OFFS = (0, 3, 1, 2)

def coords():
    arc, vec = lax.axis_index("arc"), lax.axis_index("vec")
    return (arc // 4, arc % 4, vec // 2), vec % 2

def dev(pos, core):
    return (pos[0] * 4 + pos[1], pos[2] * 2 + core)

def moved(pos, dim, off):
    return tuple((p + off) % 4 if d == dim else p for d, p in enumerate(pos))

def entry_barrier(pos, core):
    barrier = pltpu.get_barrier_semaphore()
    for dim in range(3):
        for off in (1, 3):
            pl.semaphore_signal(barrier, inc=1, device_id=dev(moved(pos, dim, off), core), device_id_type=MESH)
    pl.semaphore_signal(barrier, inc=1, device_id=dev(pos, 1 - core), device_id_type=MESH)
    return lambda: pl.semaphore_wait(barrier, 7)

def gather_all(G, send, recv, csend, crecv, pos, core):
    pend = []
    cpend = []
    nsem = [0]
    ncs = [0]
    def at(sel, cc, rows):
        return G.at[sel[0], sel[1], sel[2], cc, pl.ds(rows[0], rows[1] - rows[0])]
    def make(sel_src, dim, off, rows):
        i = nsem[0]; nsem[0] += 1
        ref = at(sel_src, core, rows)
        return pltpu.make_async_remote_copy(ref, ref, send.at[i], recv.at[i],
            device_id=dev(moved(pos, dim, off), core), device_id_type=MESH)
    def start(sel, dim, off, rows):
        c = make(sel, dim, off, rows); c.start(); pend.append(c); return c
    def cross(sel, rows):
        i = ncs[0]; ncs[0] += 1
        ref = at(sel, core, rows)
        c = pltpu.make_async_remote_copy(ref, ref, csend.at[i], crecv.at[i],
            device_id=dev(pos, 1 - core), device_id_type=MESH)
        c.start(); cpend.append(c)
    def rel(dim, off):
        return moved(pos, dim, off)
    def allof(sel, *dims):
        return tuple(slice(None) if d in dims else s for d, s in enumerate(sel))
    A = [(c[0], c[1]) for c in CUT]; B = [(c[1], c[2]) for c in CUT]; F = [(c[0], c[2]) for c in CUT]
    s1 = {}; f1 = {}; s2 = {}; f2 = {}; s3 = {}; f3 = {}
    def S2(p, o1):
        d1, d2, d3 = DIMS[p]
        for off in (1, 3):
            s2[p, o1, off] = start(moved(pos, d1, o1), d2, off, F[p])
    def S3(p, o2):
        d1, d2, d3 = DIMS[p]
        for off in (1, 3):
            s3[p, o2, off] = start(allof(moved(pos, d2, o2), d1), d3, off, F[p])
    for p in range(3):
        d1 = DIMS[p][0]
        for off in (1, 3):
            s1[p, off] = start(pos, d1, off, F[p])
    def S3one(p, o1):
        d1, d2, d3 = DIMS[p]
        for off in (1, 3):
            s3[p, 0, off, o1] = start(moved(pos, d1, o1), d3, off, F[p])
    for p in range(3):
        S2(p, 0)
    for p in range(3):
        S3one(p, 0)
    cross(pos, (0, 640))
    for p in range(3):
        d1 = DIMS[p][0]
        s1[p, 1].wait_recv()
        f1[p, 1] = start(rel(d1, 3), d1, 1, A[p])
        s1[p, 3].wait_recv()
        f1[p, 3] = start(rel(d1, 1), d1, 3, B[p])
    for p in range(3):
        S2(p, 3); S2(p, 1)
        d1 = DIMS[p][0]
        S3one(p, 3); S3one(p, 1)
        cross(rel(d1, 3), F[p]); cross(rel(d1, 1), F[p])
    for p in range(3):
        f1[p, 1].wait_recv(); f1[p, 3].wait_recv()
        S2(p, 2)
        S3one(p, 2)
        cross(rel(DIMS[p][0], 2), F[p])
    for o1 in OFFS:
        for p in range(3):
            d1, d2, d3 = DIMS[p]
            s2[p, o1, 1].wait_recv()
            f2[p, o1, 1] = start(moved(rel(d1, o1), d2, 3), d2, 1, A[p])
            s2[p, o1, 3].wait_recv()
            f2[p, o1, 3] = start(moved(rel(d1, o1), d2, 1), d2, 3, B[p])
    for p in range(3):
        d1, d2, d3 = DIMS[p]
        S3(p, 3); S3(p, 1)
        cross(allof(rel(d2, 3), d1), F[p]); cross(allof(rel(d2, 1), d1), F[p])
    for p in range(3):
        d1, d2, d3 = DIMS[p]
        for o1 in OFFS:
            f2[p, o1, 1].wait_recv(); f2[p, o1, 3].wait_recv()
        S3(p, 2)
        cross(allof(rel(d2, 2), d1), F[p])
    def arrived(p, o2, off):
        for c in ([s3[p, 0, off, o1] for o1 in OFFS] if o2 == 0 else [s3[p, o2, off]]):
            c.wait_recv()
    for o2 in OFFS:
        for p in range(3):
            d1, d2, d3 = DIMS[p]
            arrived(p, o2, 1)
            sel = allof(moved(rel(d2, o2), d3, 3), d1)
            f3[p, o2, 1] = start(sel, d3, 1, A[p])
            cross(sel, F[p])
            arrived(p, o2, 3)
            sel = allof(moved(rel(d2, o2), d3, 1), d1)
            f3[p, o2, 3] = start(sel, d3, 3, B[p])
            cross(sel, F[p])
    for o2 in OFFS:
        for p in range(3):
            d1, d2, d3 = DIMS[p]
            f3[p, o2, 1].wait_recv(); f3[p, o2, 3].wait_recv()
            cross(allof(moved(rel(d2, o2), d3, 2), d1), F[p])
    for c in cpend:
        c.wait_recv()
    for c in pend + cpend:
        c.wait_send()
    return nsem[0], ncs[0]

NS, NC = 126, 55


ORDER = (2, 1, 3, 0)
F32, BF16 = jnp.float32, jnp.bfloat16
FULL = [(c[0], c[2]) for c in CUT]; HA = [(c[0], c[1]) for c in CUT]; HB = [(c[1], c[2]) for c in CUT]

def barrier_all(pos, core):
    barrier = pltpu.get_barrier_semaphore()
    for dim in range(3):
        for off in (1, 2, 3):
            for cc in (0, 1):
                pl.semaphore_signal(barrier, inc=1, device_id=dev(moved(pos, dim, off), cc), device_id_type=MESH)
    pl.semaphore_signal(barrier, inc=1, device_id=dev(pos, 1 - core), device_id_type=MESH)
    return lambda: pl.semaphore_wait(barrier, 19)

def pieces(p):
    lo, hi = FULL[p]
    out = []
    for b in range(5):
        r0, r1 = max(lo, b * 128), min(hi, b * 128 + 128)
        if r0 < r1:
            out.append((b, r0 - b * 128, r1 - b * 128))
    return out

def rows(r):
    return pl.ds(r[0], r[1] - r[0])

def reduce_scatter(proj, tab, H, W, Q, FR, SR, send, recv, pos, core, entered):
    count = [0]
    pend = []
    tags = {}
    def ring_dim(p, lvl):
        return DIMS[p][2 - lvl]
    def hsel(p, lvl, grp, off):
        d1, d2, d3 = DIMS[p]
        sel = list(pos)
        if lvl == 0:
            sel[d1] = slice(None); sel[d2] = (pos[d2] + grp) % 4; sel[d3] = (pos[d3] + off) % 4
        elif lvl == 1:
            sel[d1] = (pos[d1] + grp) % 4; sel[d2] = (pos[d2] + off) % 4
        else:
            sel[d1] = (pos[d1] + off) % 4
        return tuple(sel)
    def rsel(p, lvl, grp):
        d1, d2, d3 = DIMS[p]
        if lvl == 0:
            return tuple(slice(None) if d == d1 else (pos[d2] + grp) % 4 for d in sorted((d1, d2)))
        if lvl == 1:
            return ((pos[d1] + grp) % 4,)
        return ()
    def wsel(p, lvl, grp, off):
        h = hsel(p, lvl, grp, off)
        return tuple(h[d] for d in sorted(DIMS[p][:2]))
    def source(p, lvl, grp, off, rr):
        if lvl == 0:
            return H.at[(*hsel(p, lvl, grp, off), rows(rr))]
        return (Q if lvl == 1 else W).at[(*wsel(p, lvl, grp, off), rows(rr))]
    def start(src, dst, p, lvl, off, tag):
        i = count[0]; count[0] += 1
        c = pltpu.make_async_remote_copy(src, dst, send.at[i], recv.at[i],
            device_id=dev(moved(pos, ring_dim(p, lvl), off), core), device_id_type=MESH)
        c.start(); pend.append(c); tags[tag] = c
    def send_f(p, lvl, grp):
        r = rsel(p, lvl, grp)
        start(source(p, lvl, grp, 2, HA[p]), FR[lvl].at[(*r, rows(HA[p]))], p, lvl, 1, ("f", p, lvl, grp, 1))
        start(source(p, lvl, grp, 2, HB[p]), FR[lvl].at[(*r, rows(HB[p]))], p, lvl, 3, ("f", p, lvl, grp, 3))
    def send_s(p, lvl, grp, off, half):
        r = rsel(p, lvl, grp)
        rr = (HA if half == 0 else HB)[p]
        start(source(p, lvl, grp, off, rr), SR[lvl].at[(0 if off == 1 else 1, *r, rows(rr))], p, lvl, off, ("s", p, lvl, grp, off, half))
    def chunks(h, r, body):
        if any(isinstance(s, slice) for s in h):
            def step(i, _):
                body(tuple(i if isinstance(s, slice) else s for s in h), tuple(i if isinstance(s, slice) else s for s in r))
                return 0
            lax.fori_loop(0, 4, step, 0)
        else:
            body(h, r)
    def fill(p, grp, off):
        def body(h, r):
            g0 = ((h[0] * 4 + h[1]) * 8 + h[2] * 2 + core) * 5
            for b, r0, r1 in pieces(p):
                rr = pl.ds(r0, r1 - r0)
                e = [tab[(g0 + b) * 4 + k] for k in range(4)]
                v = (proj[e[0], rr] + proj[e[1], rr]) + (proj[e[2], rr] + proj[e[3], rr])
                H[(*h, pl.ds(b * 128 + r0, r1 - r0))] = v
        h = hsel(p, 0, grp, off)
        chunks(h, h, body)
    def add_f(p, lvl, grp, off):
        rr = rows((HA if off == 1 else HB)[p])
        def body(h, r):
            if lvl == 0:
                H[(*h, rr)] = (H[(*h, rr)].astype(F32) + FR[0][(*r, rr)].astype(F32)).astype(BF16)
            elif lvl == 1:
                Q[(*h, rr)] = (W[(*h, rr)] + FR[1][(*r, rr)].astype(F32)).astype(BF16)
            else:
                W[(*h, rr)] = W[(*h, rr)] + FR[2][(*r, rr)]
        chunks((wsel if lvl else hsel)(p, lvl, grp, off), rsel(p, lvl, grp), body)
    def add_s(p, lvl, grp):
        rr = rows(FULL[p])
        def body(h, r):
            w = r if lvl == 0 else h
            own = H[(*h, rr)].astype(F32) if lvl == 0 else W[(*h, rr)]
            v = own + SR[lvl][(0, *r, rr)].astype(F32) + SR[lvl][(1, *r, rr)].astype(F32)
            W[(*w, rr)] = v
            if lvl == 0 and grp:
                Q[(*w, rr)] = v.astype(BF16)
        chunks((wsel if lvl else hsel)(p, lvl, grp, 0), rsel(p, lvl, grp), body)
    def middle(lvl, groups):
        for grp in groups:
            for p in range(3):
                tags["f", p, lvl, grp, 1].wait_recv()
                add_f(p, lvl, grp, 1)
                send_s(p, lvl, grp, 1, 0)
                tags["f", p, lvl, grp, 3].wait_recv()
                add_f(p, lvl, grp, 3)
                send_s(p, lvl, grp, 3, 1)
    def wait_s(p, lvl, grp):
        for off in (1, 3):
            for half in (0, 1):
                tags["s", p, lvl, grp, off, half].wait_recv()
    for grp in ORDER:
        for p in range(3):
            fill(p, grp, 2)
            if grp == ORDER[0] and p == 0:
                entered()
            send_f(p, 0, grp)
    for grp in ORDER:
        for p in range(3):
            fill(p, grp, 1)
            send_s(p, 0, grp, 1, 1)
            fill(p, grp, 3)
            send_s(p, 0, grp, 3, 0)
    middle(0, ORDER[:2])
    for grp in ORDER:
        for p in range(3):
            fill(p, grp, 0)
    middle(0, ORDER[2:])
    for grp in ORDER:
        for p in range(3):
            wait_s(p, 0, grp)
            add_s(p, 0, grp)
            for o1 in ORDER:
                if grp == 2:
                    send_f(p, 1, o1)
                elif grp == 1:
                    send_s(p, 1, o1, 1, 1)
                elif grp == 3:
                    send_s(p, 1, o1, 3, 0)
    middle(1, ORDER)
    for grp in ORDER:
        for p in range(3):
            wait_s(p, 1, grp)
            add_s(p, 1, grp)
            if grp == 2:
                send_f(p, 2, 0)
            elif grp == 1:
                send_s(p, 2, 0, 1, 1)
            elif grp == 3:
                send_s(p, 2, 0, 3, 0)
    middle(2, (0,))
    for p in range(3):
        wait_s(p, 2, 0)
    def finish():
        for c in pend:
            c.wait_send()
    assert count[0] == NR, count[0]
    def total(r0, r1):
        out = []
        for p in range(3):
            lo, hi = max(r0, FULL[p][0]), min(r1, FULL[p][1])
            if lo < hi:
                rr = pl.ds(lo, hi - lo)
                out.append(W[(*(pos[d] for d in sorted(DIMS[p][:2])), rr)] + SR[2][0, rr].astype(F32) + SR[2][1, rr].astype(F32))
        return jnp.concatenate(out, axis=0)
    return total, finish

NR = 162
def RS_SCRATCH(tb, tc):
    return [pltpu.VMEM((4, 4, 4, 640, 128), BF16), pltpu.VMEM((4, 4, 640, 128), F32), pltpu.VMEM((4, 4, 640, 128), BF16),
    pltpu.VMEM((4, 4, 640, 128), BF16), pltpu.VMEM((4, 640, 128), tb), pltpu.VMEM((640, 128), tc),
    pltpu.VMEM((2, 4, 4, 640, 128), BF16), pltpu.VMEM((2, 4, 640, 128), tb), pltpu.VMEM((2, 640, 128), tc),
    pltpu.SemaphoreType.DMA((NR,)), pltpu.SemaphoreType.DMA((NR,))]

def parts_of(half):
    a = -(-half // 24) * 8
    return ((0, a), (a, 2 * a), (2 * a, half))

def all_reduce(M, OUT, T, R0, R1, R2, send, recv, pos, core):
    half = M.shape[0] // 2
    parts = parts_of(half)
    pend = []
    def copy(src, dst, to):
        i = len(pend)
        c = pltpu.make_async_remote_copy(src, dst, send.at[i], recv.at[i], device_id=to, device_id_type=MESH)
        c.start(); pend.append(c); return c
    def part(cc, r):
        return pl.ds(pl.multiple_of(cc * half + r[0], 8), r[1] - r[0])
    def steps(p, k):
        d = DIMS[p][k]
        return pos[d], [(o, j) for o in ((2, 1, 3, 0) if k != 1 else (2, 1, 3)) for j in ((0, 1) if k != 1 else (0,)) if o or j], d
    got = {}
    def send_step(p, k):
        me, moves, d = steps(p, k)
        rr = rows(parts[p])
        slot = me * 2 + core if k == 0 else me if k == 1 else core * 4 + me
        buf = (R0, R1, R2)[k]
        buf[slot, rr] = M[part(core, parts[p])] if k == 0 else T[k - 1, rr]
        for o, j in moves:
            to = 1 - core if j else core
            src = M.at[part(to, parts[p])] if k == 0 else T.at[k - 1, rr]
            got[p, k, o, j] = copy(src, buf.at[slot, rr], dev(moved(pos, d, o), to))
    def take(p, k):
        for o, j in reversed(steps(p, k)[1]):
            got[p, k, o, j].wait_recv()
    def quad(buf, i, rr):
        return (buf[i, rr] + buf[i + 1, rr]) + (buf[i + 2, rr] + buf[i + 3, rr])
    for p in range(3):
        send_step(p, 0)
    for k in range(3):
        for p in range(3):
            rr = rows(parts[p])
            take(p, k)
            if k == 0:
                T[0, rr] = quad(R0, 0, rr) + quad(R0, 4, rr)
            elif k == 1:
                T[1, rr] = quad(R1, 0, rr)
            else:
                for h in range(2):
                    OUT[pl.ds(h * half + parts[p][0], parts[p][1] - parts[p][0])] = quad(R2, 4 * h, rr)
            if k < 2:
                send_step(p, k + 1)
    for c in pend:
        c.wait_send()
    assert len(pend) == NG, len(pend)

NG = 51
def AR_SCRATCH(R):
    return [pltpu.VMEM((R, 128), F32), pltpu.VMEM((2, R // 2, 128), F32), pltpu.VMEM((8, R // 2, 128), F32),
            pltpu.VMEM((4, R // 2, 128), F32), pltpu.VMEM((8, R // 2, 128), F32),
            pltpu.SemaphoreType.DMA((NG,)), pltpu.SemaphoreType.DMA((NG,))]

def gram(a, b):
    return lax.dot_general(a, b, (((0,), (0,)), ((), ())), precision=lax.Precision.HIGHEST, preferred_element_type=F32)

def rs_kernel(m, proj, tab, d_ref, prior, image, grams, H, W, Q, FA, FB, FC, SA, SB, SC, send, recv, M, T, R0, R1, R2, gsend, grecv):
    pos, core = coords()
    entered = barrier_all(pos, core)
    total, finish = reduce_scatter(proj, tab, H, W, Q, (FA, FB, FC), (SA, SB, SC), send, recv, pos, core, entered)
    for b in range(5):
        rr = pl.ds(b * 128, 128)
        image[rr] = prior[rr] * d_ref[rr] + total(b * 128, b * 128 + 128).T
    M[pl.ds(0, 128)] = gram(d_ref[...], image[...])
    if m > 1:
        M[pl.ds(128, 128)] = gram(image[...], image[...])
        M[pl.ds(256, 128)] = gram(d_ref[...], d_ref[...])
    all_reduce(M, grams, T, R0, R1, R2, gsend, grecv, pos, core)
    finish()

def rs_call(m, proj, tab, d, prior):
    V = pl.BlockSpec(memory_space=pltpu.VMEM)
    return pl.pallas_call(functools.partial(rs_kernel, m),
        out_shape=(jax.ShapeDtypeStruct((640, 128), F32), jax.ShapeDtypeStruct((128 * m, 128), F32)),
        in_specs=[V, pl.BlockSpec(memory_space=pltpu.SMEM), V, V], out_specs=(V, V),
        scratch_shapes=RS_SCRATCH(BF16, F32) + AR_SCRATCH(128 * m),
        compiler_params=pltpu.CompilerParams(collective_id=1 + m, has_side_effects=True, vmem_limit_bytes=36 << 20),
    )(proj, tab, d, prior)

F32, BF16 = jnp.float32, jnp.bfloat16
GROUP = 4
def nt(a, b):
    return lax.dot_general(a, b, (((1,), (1,)), ((), ())), preferred_element_type=F32).astype(BF16)
def nn(a, b):
    return lax.dot_general(a, b, (((1,), (0,)), ((), ())), preferred_element_type=F32).astype(BF16)

def k1_kernel(v_ref, idx_ref, panel_h, fac_h, proj, G, panel, fac, send, recv, csend, crecv, lsem, psend, precv):
    pos, core = coords()
    lp = pltpu.make_async_copy(panel_h, panel, lsem.at[0])
    lf = pltpu.make_async_copy(fac_h, fac, lsem.at[1])
    entered = entry_barrier(pos, core)
    lp.start(); lf.start()
    for b in range(5):
        G[pos[0], pos[1], pos[2], core, pl.ds(b * 128, 128)] = v_ref[pl.ds(b * 128, 128)].T.astype(BF16)
    entered()
    n = gather_all(G, send, recv, csend, crecv, pos, core)
    assert n == (NS, NC), n
    proj[256] = jnp.zeros((128, 128), BF16)
    lp.wait(); lf.wait()
    copies = lambda a: pltpu.make_async_remote_copy(proj.at[pl.ds(a * 8, 8)], proj.at[pl.ds(128 + a * 8, 8)],
        psend.at[a], precv.at[a], device_id=dev(pos, 1 - core), device_id_type=MESH)
    blocks = G.reshape(640, 128, 128)
    def arcs(i, _):
        mine = [i * GROUP + j for j in range(GROUP)]
        xs = [jnp.concatenate([blocks[idx_ref[a * 8 + k]] for k in range(8)], axis=1) for a in mine]
        xs = [nt(x, panel[a]) for x, a in zip(xs, mine)]
        xs = [nt(x, fac[a]) for x, a in zip(xs, mine)]
        xs = [nn(x, fac[a]) for x, a in zip(xs, mine)]
        for x, a in zip(xs, mine):
            y = nn(x, panel[a])
            for k in range(8):
                proj[a * 8 + k] = y[:, k * 128:(k + 1) * 128]
            copies(a).start()
        return 0
    lax.fori_loop(0, 16 // GROUP, arcs, 0)
    def fin(a, _):
        copies(a).wait()
        return 0
    lax.fori_loop(0, 16, fin, 0)

def k1_call(v, idx, panel, fac):
    V = pl.BlockSpec(memory_space=pltpu.VMEM); A = pl.BlockSpec(memory_space=pltpu.HBM)
    return pl.pallas_call(k1_kernel,
        out_shape=jax.ShapeDtypeStruct((257, 128, 128), BF16),
        in_specs=[V, pl.BlockSpec(memory_space=pltpu.SMEM), A, A], out_specs=V,
        scratch_shapes=[pltpu.VMEM((4, 4, 4, 2, 640, 128), BF16), pltpu.VMEM((16, 256, 1024), BF16), pltpu.VMEM((16, 256, 256), BF16),
            pltpu.SemaphoreType.DMA((NS,)), pltpu.SemaphoreType.DMA((NS,)),
            pltpu.SemaphoreType.DMA((NC,)), pltpu.SemaphoreType.DMA((NC,)), pltpu.SemaphoreType.DMA((2,)),
            pltpu.SemaphoreType.DMA((16,)), pltpu.SemaphoreType.DMA((16,))],
        compiler_params=pltpu.CompilerParams(collective_id=0, has_side_effects=True, vmem_limit_bytes=33 << 20),
    )(v, idx, pltpu.with_memory_space_constraint(panel, pltpu.HBM), pltpu.with_memory_space_constraint(fac, pltpu.HBM))

F32 = jnp.float32
def hdot(a, b, ca=1):
    return lax.dot_general(a, b, (((ca,), (0,)), ((), ())), precision=lax.Precision.HIGHEST, preferred_element_type=F32)

PIV = 16
def negated_inverses(mats):
    lane = lax.broadcasted_iota(jnp.int32, (PIV, 128), 1)
    sub = lax.broadcasted_iota(jnp.int32, (PIV, 128), 0)
    wide = lax.broadcasted_iota(jnp.int32, (128, 128), 1)
    def sweep(_, carry):
        out = []
        tops = [a[:PIV] for a in carry]
        ws = list(tops)
        for j in range(0, PIV, 2):
            for m in range(len(ws)):
                w = ws[m]
                col0 = jnp.broadcast_to(w[:, j:j + 1], (PIV, 128))
                col1 = jnp.broadcast_to(w[:, j + 1:j + 2], (PIV, 128))
                row0 = jnp.where(lane == j, 1.0, jnp.where(lane == j + 1, 0.0, jnp.broadcast_to(w[j:j + 1, :], (PIV, 128))))
                row1 = jnp.where(lane == j + 1, 1.0, jnp.where(lane == j, 0.0, jnp.broadcast_to(w[j + 1:j + 2, :], (PIV, 128))))
                a00 = jnp.broadcast_to(col0[j:j + 1, :], (PIV, 128))
                a10 = jnp.broadcast_to(col0[j + 1:j + 2, :], (PIV, 128))
                a01 = jnp.broadcast_to(col1[j:j + 1, :], (PIV, 128))
                a11 = jnp.broadcast_to(col1[j + 1:j + 2, :], (PIV, 128))
                inv = 1.0 / (a00 * a11 - a01 * a10)
                new0 = (a11 * row0 - a01 * row1) * inv
                new1 = (a00 * row1 - a10 * row0) * inv
                w = jnp.where((lane == j) | (lane == j + 1), 0.0, w) - col0 * new0 - col1 * new1
                ws[m] = jnp.where(sub == j, new0, jnp.where(sub == j + 1, new1, w))
        for a, p, w in zip(carry, tops, ws):
            m = hdot(jnp.where(lane < PIV, 0.0, p), w, 0)
            rest = jnp.where(wide < PIV, m, a - m)
            first = jnp.where(lane < PIV, -w, w)
            out.append(pltpu.roll(jnp.concatenate([rest[PIV:], first], axis=0), 128 - PIV, 1))
        return tuple(out)
    return lax.fori_loop(0, 128 // PIV, sweep, tuple(mats))

def sym(a):
    return (a + a.T) * 0.5

def first_kernel(grams, b, image, x, r, d, new):
    c, g2, g0 = grams[pl.ds(0, 128)], grams[pl.ds(128, 128)], grams[pl.ds(256, 128)]
    ci, gi = negated_inverses((sym(c), sym(g0)))
    alpha = -hdot(ci, g0)
    ca = hdot(c, alpha)
    ng = g0 - ca - ca.T + hdot(alpha, hdot(g2, alpha), 0)
    beta = -hdot(gi, ng)
    new[...] = ng
    bb = b[...]
    x[...] = hdot(bb, alpha)
    rr = bb - hdot(image[...], alpha)
    r[...] = rr
    d[...] = rr + hdot(bb, beta)

def last_kernel(c, new, x0, r0, d, image, x, r):
    (ci,) = negated_inverses((sym(c[...]),))
    alpha = -hdot(ci, new[...])
    x[...] = x0[...] + hdot(d[...], alpha)
    r[...] = r0[...] - hdot(image[...], alpha)

def first_call(grams, b, image):
    big, small = jax.ShapeDtypeStruct((640, 128), F32), jax.ShapeDtypeStruct((128, 128), F32)
    V = pl.BlockSpec(memory_space=pltpu.VMEM)
    return pl.pallas_call(first_kernel, out_shape=(big, big, big, small), in_specs=[V] * 3, out_specs=(V,) * 4,
        compiler_params=pltpu.CompilerParams(vmem_limit_bytes=16 << 20))(grams, b, image)

def last_call(c, new, x0, r0, d, image):
    big = jax.ShapeDtypeStruct((640, 128), F32)
    V = pl.BlockSpec(memory_space=pltpu.VMEM)
    return pl.pallas_call(last_kernel, out_shape=(big, big), in_specs=[V] * 6, out_specs=(V,) * 2,
        compiler_params=pltpu.CompilerParams(vmem_limit_bytes=16 << 20))(c, new, x0, r0, d, image)

def tables(owner, block, me, core):
    g = owner * 5 + block
    mine = lax.dynamic_slice_in_dim(g.reshape(128, 128), me, 1, 0).reshape(128)
    theirs = lax.dynamic_slice_in_dim(g.reshape(128, 128), me + 1 - 2 * core, 1, 0).reshape(128)
    def two(row, base):
        e = jnp.arange(128, dtype=jnp.int32)
        hit = row[None, :] == jnp.arange(640, dtype=jnp.int32)[:, None]
        first = jnp.min(jnp.where(hit, e[None], 999), axis=1)
        last = jnp.max(jnp.where(hit, e[None], -1), axis=1)
        return jnp.where(first < 999, first + base, 256), jnp.where(last > first, last + base, 256)
    t = jnp.stack([*two(mine, 0), *two(theirs, 128)], axis=1).reshape(-1).astype(jnp.int32)
    return mine, t
def per_device(right_side, prior_diag, inv_factor, coupling_panel, owner, block):
    me = lax.axis_index(("arc", "vec"))
    core = me % 2
    idx, tab = tables(owner, block, me, core)
    b = right_side.reshape(640, 128)
    prior = jnp.broadcast_to(prior_diag.reshape(640, 1), (640, 128))
    proj = k1_call(b, idx, coupling_panel, inv_factor)
    image, grams = rs_call(3, proj, tab, b, prior)
    x, r, d, new = first_call(grams, b, image)
    proj = k1_call(d, idx, coupling_panel, inv_factor)
    image, c = rs_call(1, proj, tab, d, prior)
    x, r = last_call(c, new, x, r, d, image)
    return x.reshape(5, 128, 128), r.reshape(5, 128, 128)
def solution(mesh):
    ins = (P(("arc", "vec"), None, None), P(("arc", "vec"), None), P(("arc", "vec"), None, None), P(("arc", "vec"), None, None), P(), P())
    outs = (P(("arc", "vec"), None, None), P(("arc", "vec"), None, None))
    return jax.shard_map(per_device, mesh=mesh, in_specs=ins, out_specs=outs, check_vma=False)
```
